128 devices in a mesh: blk: 4 (over x_lo, core), shard: 32 (over x_hi, y, z).
Axes of the slice: x: 4 (x_hi: 2, x_lo: 2; x = x_hi * 2 + x_lo), y: 4, z: 4, core: 2. Of those that a mesh axis runs over, the one named last changes fastest.
Arguments:
- item_features: bfloat16 [131072, 1024], P('shard'), may hold values from -6 to 6
- tower_weight: bfloat16 [1024, 512], replicated, may hold values from -0.1875 to 0.1875
- gate_in: bfloat16 [64, 128], replicated, may hold values from -0.75 to 0.75
- gate_in_bias: bfloat16 [128], replicated, may hold values from -4 to 4
- gate_out: bfloat16 [128, 64], replicated, may hold values from -0.5 to 0.5
- gate_out_bias: bfloat16 [64], replicated, may hold values from -4 to 4
- user_table: bfloat16 [16384, 512], P(('blk', 'shard')), may hold values from -6 to 6
- user_ids: int32 [512], P(('blk', 'shard')), may hold values from 0 to 127
- positive_item: int32 [512, 16], P(('blk', 'shard')), may hold values from 0 to 7167
- listed_owner: int32 [1792, 1], P(('blk', 'shard')), may hold values from 0 to 31; in each aligned block of 14 rows (0 to 13, 14 to 27, ...) at most 2 rows name the same one
- listed_slot: int32 [1792], P(('blk', 'shard')), may hold values from 0 to 31
Outputs:
- tower_gradient: float32 [1024, 512], P('shard')
- user_gradient: float32 [16384, 512], P(('blk', 'shard'))
The draws below stay inside these ranges and needn't reach their ends.
Inputs may be any that keep to these rules, and one draw needn't show every extreme that they name: `listed_owner`: at most 2 of the 14 listings of one trainer name the same owner. `user_ids`: A row of the trainer's own 128 rows of user_table. `positive_item`: A position among the rows of the user's circle.
All inputs are finite; a program needn't handle non-finite values.
Results may differ from the reference program's by a relative error of at most 0.0055.
Values may be sent and summed in bfloat16 or wider, within the bound.
No kernel may reach another device: no remote copies, remote signals or barrier semaphores. Data moves between devices by JAX's collectives and lax.ppermute only.
A program may use at most 128 MiB of HBM per device.

```python
import math
import jax
import jax.numpy as jnp
import numpy as np
from jax import lax

F = 1024
K = 8
H = 64
G = 128
BLK = 128
CAP = 2
POS = 16
OWN = 32
USERS = 4
UTAB = 128
LIST = 14
E = 512
P_SIZE = 64
GROUPS = 4
OWNERS = 32
TRAINERS = 128
CIRCLE = 7168


def plant(entries, stream_key, low, high):
    longest = entries.shape.index(max(entries.shape))
    spots = []
    for shift in (0, 1):
        where = [jax.random.randint(jax.random.fold_in(stream_key, axis), (), 0, length) for axis, length in enumerate(entries.shape)]
        where[longest] = (where[longest] + shift) % entries.shape[longest]
        spots.append(tuple(where))
    return entries.at[spots[0]].set(low).at[spots[1]].set(high)


def with_spikes(array, key, source, target, parts, factor):
    def block_of(axis_at):
        return (jnp.arange(array.shape[axis_at]) // (array.shape[axis_at] // parts)).reshape((-1,) + (1,) * (array.ndim - 1 - axis_at))

    near = jax.random.permutation(key, parts)[block_of(target)]
    far = (block_of(target) + parts // 2) % parts
    return jnp.where((block_of(source) == near) | (block_of(source) == far), factor * array, array)


def block_scale(stream_key, dims, cuts, low, high):
    loudness = 1.0
    for axis_at, parts in cuts:
        steps = jax.random.uniform(jax.random.fold_in(jax.random.fold_in(stream_key, 6), axis_at), (parts,), jnp.float32, low / len(cuts), high / len(cuts))
        loudness = loudness * jnp.repeat(jnp.exp(steps), dims[axis_at] // parts).reshape((-1,) + (1,) * (len(dims) - 1 - axis_at))
    return loudness


def assign_block(key, own, number, rows, amount, top, reach, slope):
    ranking = jax.random.permutation(key, amount)
    crowded, ordinary = shares(amount, rows * top, reach, slope, True), shares(amount, rows * top, reach, slope, False)
    places = jnp.arange(amount)

    def named(tallies, rotation):
        used = int((tallies > 0).sum())
        fixed = max(1, used // 4)
        shifted = fixed + (places - fixed + rotation * (used - fixed)) % max(1, amount - fixed)
        return jnp.zeros((amount,), jnp.int32).at[ranking[jnp.where(places < fixed, places, shifted)]].set(jnp.asarray(tallies, jnp.int32))

    tallies = jnp.where(number % 4 == 0, named(crowded, number // 4), named(ordinary, number - number // 4 - 1))
    mixed = jax.random.permutation(jax.random.fold_in(own, 3), amount)
    donor, sink = mixed[0:amount // 2 * 2:2], mixed[1:amount // 2 * 2:2]
    margin = jnp.minimum(tallies[donor] - 1, reach - tallies[sink]) // 2
    margin = jnp.where((donor == ranking[0]) | (sink == ranking[0]) | (tallies[sink] == 0), 0, jnp.maximum(margin, 0))
    shifted = jax.random.randint(jax.random.fold_in(own, 4), (amount // 2,), 0, 1 << 20) % (margin + 1)
    tallies = tallies.at[donor].add(-shifted).at[sink].add(shifted)
    labels = jnp.searchsorted(jnp.cumsum(tallies), jnp.arange(rows * top), side="right").astype(jnp.int32)
    grid = labels.reshape(top, rows).T
    grid = grid[jax.random.permutation(jax.random.fold_in(own, 1), rows)]
    rotation = jax.random.randint(jax.random.fold_in(own, 2), (rows, 1), 0, top)
    return jnp.take_along_axis(grid, (jnp.arange(top)[None, :] + rotation) % top, axis=1)


def shares(count, total, most, skew, full):
    portions = [(1 << 20) // math.isqrt(grade ** skew) + 1 for grade in range(1, count + 1)]
    largest = most if full else min(most, max(-(-total // count), total * portions[0] // sum(portions)))
    least = 1 if total - largest >= count - 1 else 0
    holding, surplus = [largest] + [least] * (count - 1), total - largest - least * (count - 1)
    while surplus > 0:
        candidates = [i for i in range(1, count) if holding[i] < largest] or [i for i in range(1, count) if holding[i] < most]
        pool, left = sum([portions[i] for i in candidates]), surplus
        for i in candidates:
            extra = min(most - holding[i], max(1, left * portions[i] // pool), surplus)
            holding[i] = holding[i] + extra
            surplus = surplus - extra
    return np.array(holding)


def noise(rng, shape, deviation, limit, split=(), kind=jnp.bfloat16):
    values = deviation * jax.random.normal(rng, shape, jnp.float32)
    if split:
        values = values * block_scale(rng, shape, split, -0.22, 0.18)
    return jnp.clip(values, -limit, limit).astype(kind)


def noise_with(rng, extent, width, limit, pieces, heavy, kind=jnp.bfloat16):
    entries = width * jax.random.normal(rng, extent, jnp.float32)
    if pieces:
        entries = entries * block_scale(rng, extent, pieces, -0.22, 0.18)
    return jnp.clip(with_spikes(entries, jax.random.fold_in(rng, 3), *heavy), -limit, limit).astype(kind)


def setup_inputs(seed: int = 0) -> dict:
    key_of = jax.random.split(jax.random.key(seed), 12)
    item_features = noise_with(key_of[0], (OWNERS * OWN * BLK, F), 1.0, 6.0, ((0, 32),), (0, 1, 32, 2.75))
    tower_weight = noise(key_of[1], (F, E), F ** -0.5, 0.1875)
    gate_in = noise(key_of[2], (P_SIZE, G), P_SIZE ** -0.5, 0.75)
    gate_in_bias = noise(key_of[3], (G,), 1.0, 4.0)
    gate_out = noise(key_of[4], (G, P_SIZE), G ** -0.5, 0.5)
    gate_out_bias = noise(key_of[5], (P_SIZE,), 1.0, 4.0)
    user_table = noise(key_of[6], (TRAINERS * UTAB, E), 1.0, 6.0, ((0, 128),))
    user_ids = plant(jax.random.randint(key_of[7], (TRAINERS * USERS,), 0, UTAB), jax.random.fold_in(key_of[7], 1), 0, UTAB - 1).astype(jnp.int32)
    positive_item = plant(jax.random.randint(key_of[8], (TRAINERS * USERS, POS), 0, CIRCLE), jax.random.fold_in(key_of[8], 1), 0, CIRCLE - 1).astype(jnp.int32)
    listed_owner_keys = jax.random.split(jax.random.fold_in(key_of[9], 1), (TRAINERS * LIST) // LIST)
    listed_owner_turns = jax.random.permutation(jax.random.fold_in(key_of[9], 3), (TRAINERS * LIST) // LIST)
    listed_owner = jax.vmap(lambda own, number: assign_block(jax.random.fold_in(key_of[9], 2), own, number, LIST, OWNERS, 1, CAP, 2))(listed_owner_keys, listed_owner_turns).reshape((TRAINERS * LIST, 1))
    listed_slot = plant(jax.random.randint(key_of[10], (TRAINERS * LIST,), 0, OWN), jax.random.fold_in(key_of[10], 1), 0, OWN - 1).astype(jnp.int32)
    return dict(item_features=item_features, tower_weight=tower_weight, gate_in=gate_in, gate_in_bias=gate_in_bias, gate_out=gate_out, gate_out_bias=gate_out_bias, user_table=user_table, user_ids=user_ids, positive_item=positive_item, listed_owner=listed_owner, listed_slot=listed_slot)


def pair_terms(user_rows, item_rows, targets, gate_in, gate_in_bias, gate_out, gate_out_bias):
    count_users = user_rows.shape[0]
    count_items = item_rows.shape[0]
    scaling = 1.0 / math.sqrt(H)
    user_parts = user_rows.astype(jnp.float32).reshape(count_users * K, H)
    item_parts = item_rows.astype(jnp.float32).reshape(count_items, K, H)
    logits = jnp.einsum('xh,ibh->xbi', user_parts, item_parts) * scaling
    logits = logits.reshape(count_users, K * K, count_items)
    gate_input = logits.astype(jnp.bfloat16)
    first_layer = gate_in.astype(jnp.float32)
    second_layer = gate_out.astype(jnp.float32)
    hidden_pre = jnp.einsum('pg,upi->ugi', first_layer, gate_input.astype(jnp.float32))
    hidden_pre = hidden_pre + gate_in_bias.astype(jnp.float32)[None, :, None]
    hidden = jax.nn.silu(hidden_pre).astype(jnp.bfloat16)
    gate_logit = jnp.einsum('gp,ugi->upi', second_layer, hidden.astype(jnp.float32))
    gate_logit = gate_logit + gate_out_bias.astype(jnp.float32)[None, :, None]
    exp_terms = jnp.exp(gate_logit)
    mixture = exp_terms / lax.optimization_barrier(jnp.sum(exp_terms, axis=1, keepdims=True))
    scores = lax.optimization_barrier(jnp.sum(mixture * logits, axis=1))
    score_grad = jax.nn.sigmoid(scores) - targets
    weighted = score_grad[:, None, :] * mixture
    logit_grad = (weighted * (logits - scores[:, None, :])).astype(jnp.bfloat16)
    gate_sig = jax.nn.sigmoid(hidden_pre)
    hidden_grad = jnp.einsum('gp,upi->ugi', second_layer, logit_grad.astype(jnp.float32))
    hidden_grad = (hidden_grad * gate_sig * (1.0 + hidden_pre * (1.0 - gate_sig))).astype(jnp.bfloat16)
    pair_grad = weighted + jnp.einsum('pg,ugi->upi', first_layer, hidden_grad.astype(jnp.float32))
    pair_grad = pair_grad.astype(jnp.bfloat16).astype(jnp.float32).reshape(count_users * K, K, count_items)
    user_delta = jnp.einsum('xbi,ibh->xh', pair_grad, item_parts).reshape(count_users, K * H) * scaling
    item_delta = jnp.einsum('xbi,xh->ibh', pair_grad, user_parts).reshape(count_items, K * H) * scaling
    return (user_delta, item_delta)

def reference(item_features, tower_weight, gate_in, gate_in_bias, gate_out, gate_out_bias, user_table, user_ids, positive_item, listed_owner, listed_slot):
    vectors = jnp.dot(item_features, tower_weight, preferred_element_type=jnp.float32).astype(jnp.bfloat16)
    vectors = vectors.reshape(OWNERS * OWN, BLK, E)
    block_ids = (listed_owner[:, 0] * OWN + listed_slot).astype(jnp.int32)
    listed = jnp.take(vectors, block_ids, axis=0).reshape(GROUPS, OWNERS, LIST * BLK, E)
    tables = user_table.reshape(TRAINERS, UTAB, E)
    row_ids = user_ids.reshape(TRAINERS, USERS).astype(jnp.int32)
    user_rows = jnp.take_along_axis(tables, row_ids[:, :, None], axis=1).reshape(GROUPS, OWNERS, USERS, E)
    targets = positive_item.reshape(GROUPS, OWNERS, USERS, POS)
    columns = jnp.arange(CIRCLE, dtype=jnp.int32)

    def column(column_index):
        col_users = lax.dynamic_index_in_dim(user_rows, column_index, 1, keepdims=False).reshape(GROUPS * USERS, E)
        col_items = lax.dynamic_index_in_dim(listed, column_index, 1, keepdims=False).reshape(CIRCLE, E)
        col_pos = lax.dynamic_index_in_dim(targets, column_index, 1, keepdims=False).reshape(GROUPS * USERS, POS)
        matches = jnp.any(col_pos[:, :, None] == columns[None, None, :], axis=1).astype(jnp.float32)
        return pair_terms(col_users, col_items, matches, gate_in, gate_in_bias, gate_out, gate_out_bias)
    user_delta, item_delta = lax.map(column, jnp.arange(OWNERS, dtype=jnp.int32))
    listing_grads = item_delta.astype(jnp.bfloat16).reshape(OWNERS, GROUPS, LIST, BLK, E)
    listing_grads = jnp.transpose(listing_grads, (1, 0, 2, 3, 4)).reshape(TRAINERS * LIST, BLK, E)
    per_block = jax.ops.segment_sum(listing_grads.astype(jnp.float32), block_ids, num_segments=OWNERS * OWN)
    per_block = per_block.reshape(OWNERS * OWN * BLK, E)
    tower_gradient = lax.dot_general(item_features.astype(jnp.float32), per_block, (((0,), (0,)), ((), ())), precision=lax.Precision.HIGHEST)
    user_deltas = jnp.transpose(user_delta.reshape(OWNERS, GROUPS, USERS, E), (1, 0, 2, 3)).reshape(TRAINERS, USERS, E)
    row_hot = (row_ids[:, :, None] == jnp.arange(UTAB, dtype=jnp.int32)[None, None, :]).astype(jnp.float32)
    user_gradient = jnp.einsum('tkr,tke->tre', row_hot, user_deltas, precision=lax.Precision.HIGHEST)
    return (tower_gradient, user_gradient.reshape(TRAINERS * UTAB, E))
```

```python
import math

import jax
import jax.numpy as jnp
from jax import lax
from jax.experimental import pallas as pl
from jax.experimental.pallas import tpu as pltpu
from jax.sharding import PartitionSpec as P

K = 8
H = 64
BLK = 128
CAP = 2
OWN = 32
USERS = 4
UTAB = 128
E = 512
GROUPS = 4
CIRCLE_USERS = GROUPS * USERS
ROWS = CIRCLE_USERS * K
PAIRS = K * K
F32 = jnp.float32
BF = jnp.bfloat16
VMEM_SPEC = pl.BlockSpec(memory_space=pltpu.VMEM)


def shifted(x, by):
    return lax.ppermute(x, "blk", [(i, (i + by) % GROUPS) for i in range(GROUPS)])


def tower_kernel(weight_t, features, out):
    product = lax.dot_general(
        weight_t[...], features[...], (((1,), (1,)), ((), ())), preferred_element_type=F32
    ).astype(BF)
    for c in range(2):
        for b in range(K):
            out[c, :, b * BLK : (b + 1) * BLK] = product[
                b * H : (b + 1) * H, c * BLK : (c + 1) * BLK
            ]


def tower_vectors(features, weight_t):
    width = features.shape[1]
    return pl.pallas_call(
        tower_kernel,
        grid=(OWN // 2,),
        in_specs=[
            pl.BlockSpec((E, width), lambda i: (0, 0)),
            pl.BlockSpec((2 * BLK, width), lambda i: (i, 0)),
        ],
        out_specs=pl.BlockSpec((2, H, K * BLK), lambda i: (i, 0, 0)),
        out_shape=jax.ShapeDtypeStruct((OWN, H, K * BLK), BF),
        compiler_params=pltpu.CompilerParams(vmem_limit_bytes=32 << 20),
        cost_estimate=pl.CostEstimate(
            flops=2 * OWN * BLK * E * width, bytes_accessed=13 << 20, transcendentals=0
        ),
        name="tower",
    )(weight_t, features)


def pair_kernel(codes, arrived, vt, first_half, first, second_t, second_half, bias1, bias2,
                user_out, grad_out, logits, pair_grad, grads, deltas):
    grads[...] = jnp.zeros_like(grads)
    deltas[...] = jnp.zeros_like(deltas)
    lane = lax.broadcasted_iota(jnp.int32, (16, BLK), 1).astype(F32)
    n = CIRCLE_USERS

    def step(position, carry):
        shard = position // CAP
        rank = position % CAP
        slot = codes[shard, rank]

        @pl.when(slot >= 0)
        def _():
            start = codes[shard, CAP + rank].astype(F32) * BLK
            packed = arrived[shard, 0 : ROWS // 2, :]
            users = jnp.concatenate([packed[:, :H], packed[:, H:]], axis=0)
            items = vt[slot]
            logits[...] = jnp.dot(users, items, preferred_element_type=F32)
            meta = arrived[shard, ROWS // 2 : ROWS // 2 + 16, :].astype(F32)
            offset = meta[:, 0:16] * BLK + meta[:, 16:32] - start
            lk = jnp.concatenate(
                [
                    jnp.concatenate(
                        [
                            logits[u * K : (u + 1) * K, b * BLK : (b + 1) * BLK]
                            for b in range(K)
                        ],
                        axis=0,
                    )
                    for u in range(n)
                ],
                axis=1,
            )
            y = jnp.concatenate(
                [
                    jnp.max(
                        jnp.where(offset[:, u : u + 1] == lane, 1.0, 0.0), axis=0, keepdims=True
                    )
                    for u in range(n)
                ],
                axis=1,
            )
            h = jnp.dot(first_half[...], lk.astype(BF), preferred_element_type=F32)
            h = h + jnp.concatenate([bias1[...]] * n, axis=1)
            t = jnp.tanh(h)
            q = 1.0 + t
            silu = h * q
            slope = q + silu * (1.0 - t)
            gate = jnp.dot(second_t[...], silu.astype(BF), preferred_element_type=F32)
            e = jnp.exp(gate + jnp.concatenate([bias2[...]] * n, axis=1))
            inverse = 1.0 / jnp.sum(e, axis=0, keepdims=True)
            score = jnp.sum(e * lk, axis=0, keepdims=True) * inverse
            score_grad = 0.5 + 0.5 * jnp.tanh(0.5 * score) - y
            weighted = e * (score_grad * inverse)
            logit_grad = (weighted * (lk - score)).astype(BF)
            hidden_grad = jnp.dot(second_half[...], logit_grad, preferred_element_type=F32)
            hidden_grad = (hidden_grad * slope).astype(BF)
            pg = jnp.dot(first[...], hidden_grad, preferred_element_type=F32) + weighted
            for b in range(K):
                pair_grad[:, b * BLK : (b + 1) * BLK] = jnp.concatenate(
                    [pg[b * K : (b + 1) * K, u * BLK : (u + 1) * BLK] for u in range(n)], axis=0
                ).astype(BF)
            pgv = pair_grad[...]
            deltas[shard] += lax.dot_general(
                pgv, items, (((1,), (1,)), ((), ())), preferred_element_type=F32
            )
            grads[slot] += jnp.dot(users.T, pgv, preferred_element_type=F32)

        return carry

    lax.fori_loop(0, codes.shape[0] * CAP, step, 0)
    scaling = 1.0 / math.sqrt(H)
    user_out[:, :, :H] = (deltas[:, : ROWS // 2, :] * scaling).astype(BF)
    user_out[:, :, H:] = (deltas[:, ROWS // 2 :, :] * scaling).astype(BF)
    grad_out[...] = grads[...].astype(BF)


def pair_terms(codes, arrived, vt, gates):
    owners = codes.shape[0]
    return pl.pallas_call(
        pair_kernel,
        out_shape=(
            jax.ShapeDtypeStruct((owners, ROWS // 2, 2 * H), BF),
            jax.ShapeDtypeStruct((OWN, H, K * BLK), BF),
        ),
        in_specs=[pl.BlockSpec(memory_space=pltpu.SMEM)] + [VMEM_SPEC] * 8,
        out_specs=(VMEM_SPEC, VMEM_SPEC),
        scratch_shapes=[
            pltpu.VMEM((ROWS, K * BLK), F32),
            pltpu.VMEM((ROWS, K * BLK), BF),
            pltpu.VMEM((OWN, H, K * BLK), F32),
            pltpu.VMEM((owners, ROWS, H), F32),
        ],
        compiler_params=pltpu.CompilerParams(vmem_limit_bytes=56 << 20),
        cost_estimate=pl.CostEstimate(
            flops=40 << 30, bytes_accessed=12 << 20, transcendentals=1 << 24
        ),
        name="pairs",
    )(codes, arrived, vt, *gates)


def tower_gradient_kernel(grads, features, out, total):
    step = pl.program_id(0)

    @pl.when(step == 0)
    def _():
        total[...] = jnp.zeros_like(total)

    left = jnp.concatenate(
        [
            jnp.concatenate([grads[c, :, b * BLK : (b + 1) * BLK] for b in range(K)], axis=0)
            for c in range(grads.shape[0])
        ],
        axis=1,
    )
    total[...] += jnp.dot(left, features[...], preferred_element_type=F32)

    @pl.when(step == pl.num_programs(0) - 1)
    def _():
        out[...] = total[...].T.astype(BF)


def tower_gradient_terms(grads, features):
    width = features.shape[1]
    blocks = 4
    return pl.pallas_call(
        tower_gradient_kernel,
        grid=(OWN // blocks,),
        in_specs=[
            pl.BlockSpec((blocks, H, K * BLK), lambda i: (i, 0, 0)),
            pl.BlockSpec((blocks * BLK, width), lambda i: (i, 0)),
        ],
        out_specs=pl.BlockSpec((width, E), lambda i: (0, 0)),
        out_shape=jax.ShapeDtypeStruct((width, E), BF),
        scratch_shapes=[pltpu.VMEM((E, width), F32)],
        compiler_params=pltpu.CompilerParams(vmem_limit_bytes=40 << 20),
        cost_estimate=pl.CostEstimate(
            flops=2 * OWN * BLK * E * width, bytes_accessed=13 << 20, transcendentals=0
        ),
        name="tower_gradient",
    )(grads, features)


def gate_layers(gate_in, gate_in_bias, gate_out, gate_out_bias):
    hidden = gate_in.shape[1]
    first = gate_in.reshape(K, K, hidden).transpose(1, 0, 2).reshape(PAIRS, hidden)
    second = gate_out.reshape(hidden, K, K).transpose(0, 2, 1).reshape(hidden, PAIRS)
    bias2 = gate_out_bias.reshape(K, K).T.reshape(PAIRS)
    half = jnp.asarray(0.5, BF)
    return (
        first.T * half,
        first,
        second.T,
        second * half,
        jnp.broadcast_to(gate_in_bias.astype(F32)[:, None] * 0.5, (hidden, BLK)),
        jnp.broadcast_to(bias2.astype(F32)[:, None], (PAIRS, BLK)),
    )


def split_product(left_bf16, right_f32):
    upper = right_f32.astype(BF)
    lower = (right_f32 - upper.astype(F32)).astype(BF)
    dims = (((0,), (0,)), ((), ()))
    first = lax.dot_general(left_bf16, upper, dims, preferred_element_type=F32)
    second = lax.dot_general(left_bf16, lower, dims, preferred_element_type=F32)
    return first + second


def shards(
    item_features,
    tower_weight,
    gate_in,
    gate_in_bias,
    gate_out,
    gate_out_bias,
    user_table,
    user_ids,
    positive_item,
    listed_owner,
    listed_slot,
):
    owner_count = lax.axis_size("shard")
    group = lax.axis_index("blk")
    listings = listed_slot.shape[0]
    owner_ids = listed_owner[:, 0]
    order = jnp.arange(listings, dtype=jnp.int32)
    same_owner = owner_ids[:, None] == owner_ids[None, :]
    earlier = order[None, :] < order[:, None]
    rank_within = jnp.sum(jnp.logical_and(same_owner, earlier), axis=1)
    owner_match = owner_ids[:, None] == jnp.arange(owner_count, dtype=jnp.int32)[None, :]
    rank_match = rank_within[:, None] == jnp.arange(CAP, dtype=jnp.int32)[None, :]
    placement = jnp.logical_and(owner_match[:, :, None], rank_match[:, None, :])
    wanted = jnp.sum(jnp.where(placement, listed_slot[:, None, None] + 1, 0), axis=0) - 1
    place = group * listings + order
    wanted_place = jnp.sum(jnp.where(placement, place[:, None, None], 0), axis=0)
    codes = jnp.concatenate([wanted, wanted_place], axis=1).astype(BF)

    row_match = user_ids[:, None] == jnp.arange(UTAB, dtype=jnp.int32)[None, :]
    user_rows = jnp.dot(row_match.astype(BF), user_table, preferred_element_type=F32)
    user_rows = (user_rows * (1.0 / math.sqrt(H))).astype(BF).reshape(USERS * K, H)
    positives = positive_item.T
    marks = jnp.concatenate([positives // BLK, positives % BLK], axis=1).astype(BF)
    own = jnp.concatenate([user_rows, jnp.pad(marks, ((0, 0), (0, H - 2 * USERS)))], axis=0)
    pieces = [own] + [shifted(own, by) for by in range(1, GROUPS)]
    rows = [piece[: USERS * K] for piece in pieces]
    marks = [piece[USERS * K :] for piece in pieces]
    packed = jnp.concatenate(
        [jnp.concatenate(rows[0:2], axis=0), jnp.concatenate(rows[2:4], axis=0)], axis=1
    )
    meta = jnp.concatenate(
        [m[:, :USERS] for m in marks] + [m[:, USERS : 2 * USERS] for m in marks], axis=1
    )
    meta = jnp.pad(meta, ((0, 0), (0, 2 * H - 2 * CIRCLE_USERS)))
    common = jnp.concatenate([packed, meta], axis=0)
    sent = jnp.broadcast_to(common[None], (owner_count,) + common.shape)
    codes = jnp.pad(
        codes[:, None, :],
        ((0, 0), (ROWS // 2, 15), (2 * CIRCLE_USERS, 2 * H - 2 * CIRCLE_USERS - 2 * CAP)),
    )
    arrived = lax.all_to_all(sent + codes, "shard", split_axis=0, concat_axis=0, tiled=True)
    asked = arrived[:, ROWS // 2, 2 * CIRCLE_USERS : 2 * CIRCLE_USERS + 2 * CAP].astype(jnp.int32)

    vt = tower_vectors(item_features, tower_weight.T)
    gates = gate_layers(gate_in, gate_in_bias, gate_out, gate_out_bias)
    user_terms, grads = pair_terms(asked, arrived, vt, gates)

    user_terms = lax.all_to_all(user_terms, "shard", split_axis=0, concat_axis=0, tiled=True)
    user_sum = jnp.sum(user_terms.astype(F32), axis=0)
    half_rows = ROWS // 4
    quarters = [
        user_sum[half_rows * (q % 2) : half_rows * (q % 2 + 1), H * (q // 2) : H * (q // 2 + 1)]
        for q in range(GROUPS)
    ]
    user_delta = quarters[0]
    for q in range(1, GROUPS):
        user_delta = user_delta + shifted(quarters[q], -q)
    user_delta = user_delta.reshape(USERS, E)
    user_gradient = split_product(row_match.astype(BF), user_delta)

    partial_value = tower_gradient_terms(grads, item_features)
    width = partial_value.shape[0]
    partial_value = lax.all_to_all(
        partial_value.reshape(owner_count, width // owner_count, E),
        "shard",
        split_axis=0,
        concat_axis=0,
        tiled=True,
    )
    tower_part = jnp.sum(partial_value.astype(F32), axis=0)
    others = [shifted(tower_part, by) for by in range(1, GROUPS)]
    by_group = [tower_part] + others
    tower_gradient = (by_group[0] + by_group[2]) + (by_group[1] + by_group[3])
    return (tower_gradient, user_gradient)


def solution(mesh):
    return jax.shard_map(
        shards,
        mesh=mesh,
        in_specs=(
            P("shard", None),
            P(),
            P(),
            P(),
            P(),
            P(),
            P(("blk", "shard"), None),
            P(("blk", "shard")),
            P(("blk", "shard"), None),
            P(("blk", "shard"), None),
            P(("blk", "shard")),
        ),
        out_specs=(P("shard", None), P(("blk", "shard"), None)),
        check_vma=False,
    )
```

```python
import math

import jax
import jax.numpy as jnp
from jax import lax
from jax.experimental import pallas as pl
from jax.experimental.pallas import tpu as pltpu
from jax.sharding import PartitionSpec as P

K = 8
H = 64
BLK = 128
CAP = 2
OWN = 32
USERS = 4
TILE_USERS = 2
UTAB = 128
E = 512
GROUPS = 4
CIRCLE_USERS = GROUPS * USERS
ROWS = CIRCLE_USERS * K
PAIRS = K * K
F32 = jnp.float32
BF = jnp.bfloat16
VMEM_SPEC = pl.BlockSpec(memory_space=pltpu.VMEM)


def shifted(x, by):
    return lax.ppermute(x, "blk", [(i, (i + by) % GROUPS) for i in range(GROUPS)])


def tower_kernel(weight_t, features, out):
    product = lax.dot_general(
        weight_t[...], features[...], (((1,), (1,)), ((), ())), preferred_element_type=F32
    ).astype(BF)
    for c in range(2):
        for b in range(K):
            out[c, :, b * BLK : (b + 1) * BLK] = product[
                b * H : (b + 1) * H, c * BLK : (c + 1) * BLK
            ]


def tower_vectors(features, weight_t):
    width = features.shape[1]
    return pl.pallas_call(
        tower_kernel,
        grid=(OWN // 2,),
        in_specs=[
            pl.BlockSpec((E, width), lambda i: (0, 0)),
            pl.BlockSpec((2 * BLK, width), lambda i: (i, 0)),
        ],
        out_specs=pl.BlockSpec((2, H, K * BLK), lambda i: (i, 0, 0)),
        out_shape=jax.ShapeDtypeStruct((OWN, H, K * BLK), BF),
        compiler_params=pltpu.CompilerParams(vmem_limit_bytes=58 << 20),
        cost_estimate=pl.CostEstimate(
            flops=2 * OWN * BLK * E * width, bytes_accessed=13 << 20, transcendentals=0
        ),
        name="tower",
    )(weight_t, features)


def pair_kernel(codes, arrived_any, vt_any, features_any, first_half, first, second_t,
                second_half, bias1, bias2, out, arrived, vt, features, grads, deltas, total,
                entry_slot, entry_shard, entry_start, sems, *buffers):
    copies = [
        pltpu.make_async_copy(source, target, sems.at[i])
        for i, (source, target) in enumerate(
            ((arrived_any, arrived), (vt_any, vt), (features_any, features))
        )
    ]
    for copy in copies:
        copy.start()
    owners = codes.shape[0]
    logits, hidden, slope, weights, back, pair_grad = [
        buffers[2 * i : 2 * i + 2] for i in range(6)
    ]
    tile = TILE_USERS * BLK
    tiles = CIRCLE_USERS // TILE_USERS

    def clear(position, carry):
        entry_slot[position] = OWN
        entry_shard[position] = owners
        entry_start[position] = 0
        return carry

    lax.fori_loop(0, owners * CAP + 8, clear, 0)

    def enter(position, count):
        shard = position // CAP
        rank = position % CAP
        slot = codes[shard, rank]
        entry_slot[count + 2] = jnp.where(slot >= 0, slot, OWN)
        entry_shard[count + 2] = jnp.where(slot >= 0, shard, owners)
        entry_start[count + 2] = codes[shard, CAP + rank] * BLK
        return count + jnp.where(slot >= 0, 1, 0)

    count = lax.fori_loop(0, owners * CAP, enter, 0)
    grads[...] = jnp.zeros_like(grads)
    deltas[...] = jnp.zeros_like(deltas)
    lane = lax.broadcasted_iota(jnp.int32, (16, BLK), 1).astype(F32)
    copies[0].wait()
    copies[1].wait()

    def users_of(shard):
        packed = arrived[jnp.minimum(shard, owners - 1), 0 : ROWS // 2, :]
        return jnp.concatenate([packed[:, :H], packed[:, H:]], axis=0)

    def items_of(slot):
        return vt[jnp.minimum(slot, OWN - 1)]

    def logits_of(ref, k):
        return jnp.concatenate(
            [
                jnp.concatenate(
                    [ref[u * K : (u + 1) * K, b * BLK : (b + 1) * BLK] for b in range(K)],
                    axis=0,
                )
                for u in range(TILE_USERS * k, TILE_USERS * (k + 1))
            ],
            axis=1,
        )

    def stages(n, even):
        odd = 1 - even
        start_slot, start_shard = entry_slot[n + 2], entry_shard[n + 2]
        middle_shard, middle_start = entry_shard[n + 1], entry_start[n + 1]
        end_slot, end_shard = entry_slot[n], entry_shard[n]
        meta = arrived[jnp.minimum(middle_shard, owners - 1), ROWS // 2 : ROWS // 2 + 16, :]
        meta = meta.astype(F32)
        offset = meta[:, 0:16] * BLK + meta[:, 16:32] - middle_start.astype(F32)

        def scores():
            logits[even][...] = jnp.dot(
                users_of(start_shard), items_of(start_slot), preferred_element_type=F32
            )

        def forward(k):
            columns = slice(k * tile, (k + 1) * tile)
            h = jnp.dot(
                first_half[...],
                logits_of(logits[even], k).astype(BF),
                preferred_element_type=F32,
            ) + jnp.concatenate([bias1[...]] * TILE_USERS, axis=1)
            t = jnp.tanh(h)
            q = 1.0 + t
            silu = h * q
            hidden[even][:, columns] = silu.astype(BF)
            slope[even][:, columns] = q + silu * (1.0 - t)

        def mix(k):
            columns = slice(k * tile, (k + 1) * tile)
            users = range(TILE_USERS * k, TILE_USERS * (k + 1))
            y = jnp.concatenate(
                [
                    jnp.max(
                        jnp.where(offset[:, u : u + 1] == lane, 1.0, 0.0), axis=0, keepdims=True
                    )
                    for u in users
                ],
                axis=1,
            )
            gate = jnp.dot(
                second_t[...], hidden[odd][:, columns], preferred_element_type=F32
            ) + jnp.concatenate([bias2[...]] * TILE_USERS, axis=1)
            e = jnp.exp(gate)
            lk = logits_of(logits[odd], k)
            inverse = 1.0 / jnp.sum(e, axis=0, keepdims=True)
            score = jnp.sum(e * lk, axis=0, keepdims=True) * inverse
            score_grad = 0.5 + 0.5 * jnp.tanh(0.5 * score) - y
            weighted = e * (score_grad * inverse)
            weights[odd][:, columns] = weighted
            return (weighted * (lk - score)).astype(BF)

        def gate_back(k, logit_grad):
            columns = slice(k * tile, (k + 1) * tile)
            hidden_grad = jnp.dot(second_half[...], logit_grad, preferred_element_type=F32)
            back[odd][:, columns] = (hidden_grad * slope[odd][:, columns]).astype(BF)

        def pair_back(k):
            columns = slice(k * tile, (k + 1) * tile)
            pg = jnp.dot(first[...], back[even][:, columns], preferred_element_type=F32)
            pg = pg + weights[even][:, columns]
            rows = slice(K * TILE_USERS * k, K * TILE_USERS * (k + 1))
            for b in range(K):
                pair_grad[even][rows, b * BLK : (b + 1) * BLK] = jnp.concatenate(
                    [
                        pg[b * K : (b + 1) * K, w * BLK : (w + 1) * BLK]
                        for w in range(TILE_USERS)
                    ],
                    axis=0,
                ).astype(BF)

        previous = None
        for k in range(tiles):
            pair_back(k)
            logit_grad = mix(k)
            if k == 0:
                scores()
            else:
                gate_back(k - 1, previous)
            if k >= tiles // 2:
                forward(2 * k - tiles)
                forward(2 * k - tiles + 1)
            previous = logit_grad
        gate_back(tiles - 1, previous)
        pgv = pair_grad[even][...]
        deltas[end_shard] += lax.dot_general(
            pgv, items_of(end_slot), (((1,), (1,)), ((), ())), preferred_element_type=F32
        )
        grads[end_slot] += jnp.dot(users_of(end_shard).T, pgv, preferred_element_type=F32)

    def step(i, carry):
        stages(2 * i, 0)
        stages(2 * i + 1, 1)
        return carry

    lax.fori_loop(0, (count + 3) // 2, step, 0)

    rows = out.shape[1] - ROWS // 8
    scaling = 1.0 / math.sqrt(H)
    for c in range(4):
        for half in range(2):
            first_row = half * (ROWS // 2) + c * (ROWS // 8)
            out[:, rows:, c * 2 * H + half * H : c * 2 * H + (half + 1) * H] = (
                deltas[0:owners, first_row : first_row + ROWS // 8, :] * scaling
            ).astype(BF)
    copies[2].wait()
    blocks = 4

    def add(i, carry):
        left = jnp.concatenate(
            [
                jnp.concatenate(
                    [
                        grads[i * blocks + c, :, b * BLK : (b + 1) * BLK].astype(BF)
                        for b in range(K)
                    ],
                    axis=0,
                )
                for c in range(blocks)
            ],
            axis=1,
        )
        start = pl.multiple_of(i * blocks * BLK, blocks * BLK)
        product = jnp.dot(
            left, features[pl.ds(start, blocks * BLK), :], preferred_element_type=F32
        )

        @pl.when(i == 0)
        def _():
            total[...] = product

        @pl.when(i > 0)
        def _():
            total[...] += product

        return carry

    lax.fori_loop(0, OWN // blocks, add, 0)
    for part in range(total.shape[1] // BLK):
        turned = total[:, part * BLK : (part + 1) * BLK].T.astype(BF)
        for c in range(BLK // rows):
            out[part * (BLK // rows) + c, 0:rows, :] = turned[c * rows : (c + 1) * rows, :]


def pair_terms(codes, arrived, vt, features, gates):
    owners = codes.shape[0]
    width = features.shape[1]
    any_spec = pl.BlockSpec(memory_space=pl.ANY)
    columns = CIRCLE_USERS * BLK
    hidden = gates[0].shape[0]

    def twice(shape, dtype):
        return [pltpu.VMEM(shape, dtype)] * 2

    return pl.pallas_call(
        pair_kernel,
        out_shape=jax.ShapeDtypeStruct((owners, width // owners + ROWS // 8, E), BF),
        in_specs=[pl.BlockSpec(memory_space=pltpu.SMEM)] + [any_spec] * 3 + [VMEM_SPEC] * 6,
        out_specs=VMEM_SPEC,
        scratch_shapes=[
            pltpu.VMEM(arrived.shape, BF),
            pltpu.VMEM(vt.shape, BF),
            pltpu.VMEM(features.shape, BF),
            pltpu.VMEM((OWN + 1, H, K * BLK), F32),
            pltpu.VMEM((owners + 1, ROWS, H), F32),
            pltpu.VMEM((E, width), F32),
            pltpu.SMEM((owners * CAP + 8,), jnp.int32),
            pltpu.SMEM((owners * CAP + 8,), jnp.int32),
            pltpu.SMEM((owners * CAP + 8,), jnp.int32),
            pltpu.SemaphoreType.DMA((3,)),
        ]
        + twice((ROWS, K * BLK), F32)
        + twice((hidden, columns), BF)
        + twice((hidden, columns), F32)
        + twice((PAIRS, columns), F32)
        + twice((hidden, columns), BF)
        + twice((ROWS, K * BLK), BF),
        compiler_params=pltpu.CompilerParams(vmem_limit_bytes=58 << 20),
        cost_estimate=pl.CostEstimate(
            flops=40 << 30, bytes_accessed=16 << 20, transcendentals=1 << 24
        ),
        name="pairs",
    )(codes, arrived, vt, features, *gates)


def gate_layers(gate_in, gate_in_bias, gate_out, gate_out_bias):
    hidden = gate_in.shape[1]
    first = gate_in.reshape(K, K, hidden).transpose(1, 0, 2).reshape(PAIRS, hidden)
    second = gate_out.reshape(hidden, K, K).transpose(0, 2, 1).reshape(hidden, PAIRS)
    bias2 = gate_out_bias.reshape(K, K).T.reshape(PAIRS)
    half = jnp.asarray(0.5, BF)
    return (
        first.T * half,
        first,
        second.T,
        second * half,
        jnp.broadcast_to(gate_in_bias.astype(F32)[:, None] * 0.5, (hidden, BLK)),
        jnp.broadcast_to(bias2.astype(F32)[:, None], (PAIRS, BLK)),
    )


def split_product(left_bf16, right_f32):
    upper = right_f32.astype(BF)
    lower = (right_f32 - upper.astype(F32)).astype(BF)
    dims = (((0,), (0,)), ((), ()))
    first = lax.dot_general(left_bf16, upper, dims, preferred_element_type=F32)
    second = lax.dot_general(left_bf16, lower, dims, preferred_element_type=F32)
    return first + second


def shards(
    item_features,
    tower_weight,
    gate_in,
    gate_in_bias,
    gate_out,
    gate_out_bias,
    user_table,
    user_ids,
    positive_item,
    listed_owner,
    listed_slot,
):
    owner_count = lax.axis_size("shard")
    group = lax.axis_index("blk")
    listings = listed_slot.shape[0]
    owner_ids = listed_owner[:, 0]
    order = jnp.arange(listings, dtype=jnp.int32)
    same_owner = owner_ids[:, None] == owner_ids[None, :]
    earlier = order[None, :] < order[:, None]
    rank_within = jnp.sum(jnp.logical_and(same_owner, earlier), axis=1)
    owner_match = owner_ids[:, None] == jnp.arange(owner_count, dtype=jnp.int32)[None, :]
    rank_match = rank_within[:, None] == jnp.arange(CAP, dtype=jnp.int32)[None, :]
    placement = jnp.logical_and(owner_match[:, :, None], rank_match[:, None, :])
    wanted = jnp.sum(jnp.where(placement, listed_slot[:, None, None] + 1, 0), axis=0) - 1
    place = group * listings + order
    wanted_place = jnp.sum(jnp.where(placement, place[:, None, None], 0), axis=0)
    codes = jnp.concatenate([wanted, wanted_place], axis=1).astype(BF)

    row_match = user_ids[:, None] == jnp.arange(UTAB, dtype=jnp.int32)[None, :]
    user_rows = jnp.dot(row_match.astype(BF), user_table, preferred_element_type=F32)
    user_rows = (user_rows * (1.0 / math.sqrt(H))).astype(BF).reshape(USERS * K, H)
    positives = positive_item.T
    marks = jnp.concatenate([positives // BLK, positives % BLK], axis=1).astype(BF)
    own = jnp.concatenate([user_rows, jnp.pad(marks, ((0, 0), (0, H - 2 * USERS)))], axis=0)
    pieces = [own] + [shifted(own, by) for by in range(1, GROUPS)]
    rows = [piece[: USERS * K] for piece in pieces]
    marks = [piece[USERS * K :] for piece in pieces]
    packed = jnp.concatenate(
        [jnp.concatenate(rows[0:2], axis=0), jnp.concatenate(rows[2:4], axis=0)], axis=1
    )
    meta = jnp.concatenate(
        [m[:, :USERS] for m in marks] + [m[:, USERS : 2 * USERS] for m in marks], axis=1
    )
    meta = jnp.pad(meta, ((0, 0), (0, 2 * H - 2 * CIRCLE_USERS)))
    common = jnp.concatenate([packed, meta], axis=0)
    sent = jnp.broadcast_to(common[None], (owner_count,) + common.shape)
    codes = jnp.pad(
        codes[:, None, :],
        ((0, 0), (ROWS // 2, 15), (2 * CIRCLE_USERS, 2 * H - 2 * CIRCLE_USERS - 2 * CAP)),
    )
    arrived = lax.all_to_all(sent + codes, "shard", split_axis=0, concat_axis=0, tiled=True)
    asked = arrived[:, ROWS // 2, 2 * CIRCLE_USERS : 2 * CIRCLE_USERS + 2 * CAP].astype(jnp.int32)

    vt = tower_vectors(item_features, tower_weight.T)
    gates = gate_layers(gate_in, gate_in_bias, gate_out, gate_out_bias)
    terms = pair_terms(asked, arrived, vt, item_features, gates)
    terms = lax.all_to_all(terms, "shard", split_axis=0, concat_axis=0, tiled=True)
    sums = jnp.sum(terms.astype(F32), axis=0)
    rows = sums.shape[0] - ROWS // 8
    user_sum = sums[rows:].reshape(ROWS // 8, 4, 2 * H).transpose(1, 0, 2)
    user_sum = user_sum.reshape(ROWS // 2, 2 * H)
    half_rows = ROWS // 4
    quarters = [
        user_sum[
            half_rows * (q % 2) : half_rows * (q % 2 + 1), H * (q // 2) : H * (q // 2 + 1)
        ].reshape(USERS, E)
        for q in range(GROUPS)
    ]
    parts = [jnp.concatenate([sums[:rows], quarter], axis=0) for quarter in quarters]
    parts = [parts[0]] + [shifted(parts[q], -q) for q in range(1, GROUPS)]
    total = (parts[0] + parts[2]) + (parts[1] + parts[3])
    tower_gradient = total[:rows]
    user_gradient = split_product(row_match.astype(BF), total[rows:])
    return (tower_gradient, user_gradient)


def solution(mesh):
    return jax.shard_map(
        shards,
        mesh=mesh,
        in_specs=(
            P("shard", None),
            P(),
            P(),
            P(),
            P(),
            P(),
            P(("blk", "shard"), None),
            P(("blk", "shard")),
            P(("blk", "shard"), None),
            P(("blk", "shard"), None),
            P(("blk", "shard")),
        ),
        out_specs=(P("shard", None), P(("blk", "shard"), None)),
        check_vma=False,
    )
```

```python
import math

import jax
import jax.numpy as jnp
from jax import lax
from jax.experimental import pallas as pl
from jax.experimental.pallas import tpu as pltpu
from jax.sharding import PartitionSpec as P

K = 8
H = 64
BLK = 128
CAP = 2
OWN = 32
USERS = 4
TILE_USERS = 2
UTAB = 128
E = 512
GROUPS = 4
CIRCLE_USERS = GROUPS * USERS
ROWS = CIRCLE_USERS * K
PAIRS = K * K
F32 = jnp.float32
BF = jnp.bfloat16
VMEM_SPEC = pl.BlockSpec(memory_space=pltpu.VMEM)


def swapped(x, by):
    return lax.ppermute(x, "blk", [(i, i ^ by) for i in range(GROUPS)])


def tower_kernel(weight_t, features, out):
    product = lax.dot_general(
        weight_t[...], features[...], (((1,), (1,)), ((), ())), preferred_element_type=F32
    ).astype(BF)
    for c in range(out.shape[0]):
        for b in range(K):
            out[c, :, b * BLK : (b + 1) * BLK] = product[
                b * H : (b + 1) * H, c * BLK : (c + 1) * BLK
            ]


def tower_vectors(features, weight_t):
    width = features.shape[1]
    blocks = 8
    return pl.pallas_call(
        tower_kernel,
        grid=(OWN // blocks,),
        in_specs=[
            pl.BlockSpec((E, width), lambda i: (0, 0)),
            pl.BlockSpec((blocks * BLK, width), lambda i: (i, 0)),
        ],
        out_specs=pl.BlockSpec((blocks, H, K * BLK), lambda i: (i, 0, 0)),
        out_shape=jax.ShapeDtypeStruct((OWN, H, K * BLK), BF),
        compiler_params=pltpu.CompilerParams(vmem_limit_bytes=58 << 20),
        cost_estimate=pl.CostEstimate(
            flops=2 * OWN * BLK * E * width, bytes_accessed=13 << 20, transcendentals=0
        ),
        name="tower",
    )(weight_t, features)


def pair_kernel(codes, group, arrived_any, vt_any, features_any, gate_in, gate_in_bias,
                gate_out, gate_out_bias, keep, send, first_half, first, second_t, second_half,
                bias1, bias2, arrived, vt, features, grads, deltas, total,
                entry_slot, entry_shard, entry_start, sems, *buffers):
    copies = [
        pltpu.make_async_copy(source, target, sems.at[i])
        for i, (source, target) in enumerate(
            ((arrived_any, arrived), (vt_any, vt), (features_any, features))
        )
    ]
    for copy in copies:
        copy.start()
    owners = codes.shape[0]
    logits, hidden, slope, weights, back, pair_grad = [
        buffers[2 * i : 2 * i + 2] for i in range(6)
    ]
    tile = TILE_USERS * BLK
    tiles = CIRCLE_USERS // TILE_USERS

    def clear(position, carry):
        entry_slot[position] = OWN
        entry_shard[position] = owners
        entry_start[position] = 0
        return carry

    lax.fori_loop(0, owners * CAP + 8, clear, 0)

    def enter(position, count):
        shard = position // CAP
        rank = position % CAP
        slot = codes[shard, rank]
        entry_slot[count + 2] = jnp.where(slot >= 0, slot, OWN)
        entry_shard[count + 2] = jnp.where(slot >= 0, shard, owners)
        entry_start[count + 2] = codes[shard, CAP + rank] * BLK
        return count + jnp.where(slot >= 0, 1, 0)

    count = lax.fori_loop(0, owners * CAP, enter, 0)
    grads[...] = jnp.zeros_like(grads)
    deltas[...] = jnp.zeros_like(deltas)
    lane = lax.broadcasted_iota(jnp.int32, (16, BLK), 1).astype(F32)
    row = lax.broadcasted_iota(jnp.int32, (PAIRS, PAIRS), 0)
    column = lax.broadcasted_iota(jnp.int32, (PAIRS, PAIRS), 1)
    order = jnp.where(column == (row & (K - 1)) * K + (row >> 3), 1.0, 0.0).astype(BF)
    across = (((1,), (1,)), ((), ()))
    turned_in = jnp.dot(order, gate_in[...], preferred_element_type=F32)
    turned_out = lax.dot_general(order, gate_out[...], across, preferred_element_type=F32)
    first[...] = turned_in.astype(BF)
    first_half[...] = (turned_in.T * 0.5).astype(BF)
    second_t[...] = turned_out.astype(BF)
    second_half[...] = (turned_out.T * 0.5).astype(BF)
    bias1[...] = jnp.broadcast_to(gate_in_bias[...].astype(F32) * 0.5, bias1.shape).T
    bias2[...] = lax.dot_general(
        order,
        jnp.broadcast_to(gate_out_bias[...], (BLK, PAIRS)),
        across,
        preferred_element_type=F32,
    )
    copies[0].wait()
    copies[1].wait()

    def users_of(shard):
        packed = arrived[jnp.minimum(shard, owners - 1), 0 : ROWS // 2, :]
        return jnp.concatenate([packed[:, :H], packed[:, H:]], axis=0)

    def items_of(slot):
        return vt[jnp.minimum(slot, OWN - 1)]

    def logits_of(ref, k):
        return jnp.concatenate(
            [
                jnp.concatenate(
                    [ref[u * K : (u + 1) * K, b * BLK : (b + 1) * BLK] for b in range(K)],
                    axis=0,
                )
                for u in range(TILE_USERS * k, TILE_USERS * (k + 1))
            ],
            axis=1,
        )

    def stages(n, even):
        odd = 1 - even
        start_slot, start_shard = entry_slot[n + 2], entry_shard[n + 2]
        middle_shard, middle_start = entry_shard[n + 1], entry_start[n + 1]
        end_slot, end_shard = entry_slot[n], entry_shard[n]
        meta = arrived[jnp.minimum(middle_shard, owners - 1), ROWS // 2 : ROWS // 2 + 16, :]
        meta = meta.astype(F32)
        offset = meta[:, 0:16] * BLK + meta[:, 16:32] - middle_start.astype(F32)

        def scores():
            logits[even][...] = jnp.dot(
                users_of(start_shard), items_of(start_slot), preferred_element_type=F32
            )

        def forward(k):
            columns = slice(k * tile, (k + 1) * tile)
            h = jnp.dot(
                first_half[...],
                logits_of(logits[even], k).astype(BF),
                preferred_element_type=F32,
            ) + jnp.concatenate([bias1[...]] * TILE_USERS, axis=1)
            t = jnp.tanh(h)
            q = 1.0 + t
            silu = h * q
            hidden[even][:, columns] = silu.astype(BF)
            slope[even][:, columns] = q + silu * (1.0 - t)

        def mix(k):
            columns = slice(k * tile, (k + 1) * tile)
            users = range(TILE_USERS * k, TILE_USERS * (k + 1))
            y = jnp.concatenate(
                [
                    jnp.max(
                        jnp.where(offset[:, u : u + 1] == lane, 1.0, 0.0), axis=0, keepdims=True
                    )
                    for u in users
                ],
                axis=1,
            )
            gate = jnp.dot(
                second_t[...], hidden[odd][:, columns], preferred_element_type=F32
            ) + jnp.concatenate([bias2[...]] * TILE_USERS, axis=1)
            e = jnp.exp(gate)
            lk = logits_of(logits[odd], k)
            inverse = 1.0 / jnp.sum(e, axis=0, keepdims=True)
            score = jnp.sum(e * lk, axis=0, keepdims=True) * inverse
            score_grad = 0.5 + 0.5 * jnp.tanh(0.5 * score) - y
            weighted = e * (score_grad * inverse)
            weights[odd][:, columns] = weighted
            return (weighted * (lk - score)).astype(BF)

        def gate_back(k, logit_grad):
            columns = slice(k * tile, (k + 1) * tile)
            hidden_grad = jnp.dot(second_half[...], logit_grad, preferred_element_type=F32)
            back[odd][:, columns] = (hidden_grad * slope[odd][:, columns]).astype(BF)

        def pair_back(k):
            columns = slice(k * tile, (k + 1) * tile)
            pg = jnp.dot(first[...], back[even][:, columns], preferred_element_type=F32)
            pg = pg + weights[even][:, columns]
            rows = slice(K * TILE_USERS * k, K * TILE_USERS * (k + 1))
            for b in range(K):
                pair_grad[even][rows, b * BLK : (b + 1) * BLK] = jnp.concatenate(
                    [
                        pg[b * K : (b + 1) * K, w * BLK : (w + 1) * BLK]
                        for w in range(TILE_USERS)
                    ],
                    axis=0,
                ).astype(BF)

        for k in range(tiles):
            pair_back(k)
        scores()
        logit_grads = [mix(k) for k in range(tiles)]
        pgv = pair_grad[even][...]
        deltas[end_shard] += lax.dot_general(
            pgv, items_of(end_slot), (((1,), (1,)), ((), ())), preferred_element_type=F32
        )
        grads[end_slot] += jnp.dot(users_of(end_shard).T, pgv, preferred_element_type=F32)
        for k in range(tiles):
            forward(k)
            gate_back(k, logit_grads[k])

    def step(i, carry):
        stages(2 * i, 0)
        stages(2 * i + 1, 1)
        return carry

    lax.fori_loop(0, (count + 3) // 2, step, 0)

    rows = keep.shape[1] - K
    scaling = 1.0 / math.sqrt(H)
    piece = USERS * K
    for c in range(2 * USERS):
        columns = slice(c * H, (c + 1) * H)
        first_row = 2 * piece * (c // USERS) + K * (c % USERS)
        keep[:, rows:, columns] = deltas[0:owners, first_row : first_row + K, :] * scaling
        first_row = first_row + piece
        send[:, rows:, columns] = (
            deltas[0:owners, first_row : first_row + K, :] * scaling
        ).astype(BF)
    copies[2].wait()
    blocks = 4

    def add(i, carry):
        left = jnp.concatenate(
            [
                jnp.concatenate(
                    [
                        grads[i * blocks + c, :, b * BLK : (b + 1) * BLK].astype(BF)
                        for b in range(K)
                    ],
                    axis=0,
                )
                for c in range(blocks)
            ],
            axis=1,
        )
        start = pl.multiple_of(i * blocks * BLK, blocks * BLK)
        product = jnp.dot(
            left, features[pl.ds(start, blocks * BLK), :], preferred_element_type=F32
        )

        @pl.when(i == 0)
        def _():
            total[...] = product

        @pl.when(i > 0)
        def _():
            total[...] += product

        return carry

    lax.fori_loop(0, OWN // blocks, add, 0)
    parity = group[0] & 1
    for part in range(total.shape[1] // BLK):
        turned = total[:, part * BLK : (part + 1) * BLK].T
        for c in range(BLK // (2 * rows)):
            lower = turned[2 * rows * c : 2 * rows * c + rows, :]
            upper = turned[2 * rows * c + rows : 2 * rows * (c + 1), :]
            owner = part * (BLK // (2 * rows)) + c
            keep[owner, 0:rows, :] = jnp.where(parity == 0, lower, upper)
            send[owner, 0:rows, :] = jnp.where(parity == 0, upper, lower).astype(BF)


def pair_terms(codes, group, arrived, vt, features, gates):
    owners = codes.shape[0]
    width = features.shape[1]
    any_spec = pl.BlockSpec(memory_space=pl.ANY)
    columns = CIRCLE_USERS * BLK
    hidden = gates[0].shape[1]
    shape = (owners, width // (2 * owners) + K, E)
    smem = pl.BlockSpec(memory_space=pltpu.SMEM)

    def twice(shape, dtype):
        return [pltpu.VMEM(shape, dtype)] * 2

    return pl.pallas_call(
        pair_kernel,
        out_shape=(jax.ShapeDtypeStruct(shape, F32), jax.ShapeDtypeStruct(shape, BF)),
        in_specs=[smem] * 2 + [any_spec] * 3 + [VMEM_SPEC] * 4,
        out_specs=(VMEM_SPEC, VMEM_SPEC),
        scratch_shapes=[
            pltpu.VMEM((hidden, PAIRS), BF),
            pltpu.VMEM((PAIRS, hidden), BF),
            pltpu.VMEM((PAIRS, hidden), BF),
            pltpu.VMEM((hidden, PAIRS), BF),
            pltpu.VMEM((hidden, BLK), F32),
            pltpu.VMEM((PAIRS, BLK), F32),
            pltpu.VMEM(arrived.shape, BF),
            pltpu.VMEM(vt.shape, BF),
            pltpu.VMEM(features.shape, BF),
            pltpu.VMEM((OWN + 1, H, K * BLK), F32),
            pltpu.VMEM((owners + 1, ROWS, H), F32),
            pltpu.VMEM((E, width), F32),
            pltpu.SMEM((owners * CAP + 8,), jnp.int32),
            pltpu.SMEM((owners * CAP + 8,), jnp.int32),
            pltpu.SMEM((owners * CAP + 8,), jnp.int32),
            pltpu.SemaphoreType.DMA((3,)),
        ]
        + twice((ROWS, K * BLK), F32)
        + twice((hidden, columns), BF)
        + twice((hidden, columns), F32)
        + twice((PAIRS, columns), F32)
        + twice((hidden, columns), BF)
        + twice((ROWS, K * BLK), BF),
        compiler_params=pltpu.CompilerParams(vmem_limit_bytes=58 << 20),
        cost_estimate=pl.CostEstimate(
            flops=40 << 30, bytes_accessed=16 << 20, transcendentals=1 << 24
        ),
        name="pairs",
    )(codes, group, arrived, vt, features, *gates)


def split_product(left_bf16, right_f32):
    upper = right_f32.astype(BF)
    lower = (right_f32 - upper.astype(F32)).astype(BF)
    dims = (((0,), (0,)), ((), ()))
    first = lax.dot_general(left_bf16, upper, dims, preferred_element_type=F32)
    second = lax.dot_general(left_bf16, lower, dims, preferred_element_type=F32)
    return first + second


def shards(
    item_features,
    tower_weight,
    gate_in,
    gate_in_bias,
    gate_out,
    gate_out_bias,
    user_table,
    user_ids,
    positive_item,
    listed_owner,
    listed_slot,
):
    owner_count = lax.axis_size("shard")
    group = lax.axis_index("blk")
    listings = listed_slot.shape[0]
    owner_ids = listed_owner[:, 0]
    order = jnp.arange(listings, dtype=jnp.int32)
    same_owner = owner_ids[:, None] == owner_ids[None, :]
    earlier = order[None, :] < order[:, None]
    rank_within = jnp.sum(jnp.logical_and(same_owner, earlier), axis=1)
    owner_match = owner_ids[:, None] == jnp.arange(owner_count, dtype=jnp.int32)[None, :]
    rank_match = rank_within[:, None] == jnp.arange(CAP, dtype=jnp.int32)[None, :]
    placement = jnp.logical_and(owner_match[:, :, None], rank_match[:, None, :])
    wanted = jnp.sum(jnp.where(placement, listed_slot[:, None, None] + 1, 0), axis=0) - 1
    place = group * listings + order
    wanted_place = jnp.sum(jnp.where(placement, place[:, None, None], 0), axis=0)
    codes = jnp.concatenate([wanted, wanted_place], axis=1).astype(BF)

    row_match = user_ids[:, None] == jnp.arange(UTAB, dtype=jnp.int32)[None, :]
    user_rows = jnp.dot(row_match.astype(BF), user_table, preferred_element_type=F32)
    user_rows = (user_rows * (1.0 / math.sqrt(H))).astype(BF).reshape(USERS * K, H)
    positives = positive_item.T
    marks = jnp.concatenate([positives // BLK, positives % BLK], axis=1).astype(BF)
    own = jnp.concatenate([user_rows, jnp.pad(marks, ((0, 0), (0, H - 2 * USERS)))], axis=0)
    pieces = [own] + [swapped(own, by) for by in range(1, GROUPS)]
    rows = [piece[: USERS * K] for piece in pieces]
    marks = [piece[USERS * K :] for piece in pieces]
    packed = jnp.concatenate(
        [jnp.concatenate(rows[0:2], axis=0), jnp.concatenate(rows[2:4], axis=0)], axis=1
    )
    meta = jnp.concatenate(
        [m[:, :USERS] for m in marks] + [m[:, USERS : 2 * USERS] for m in marks], axis=1
    )
    meta = jnp.pad(meta, ((0, 0), (0, 2 * H - 2 * CIRCLE_USERS)))
    common = jnp.concatenate([packed, meta], axis=0)
    sent = jnp.broadcast_to(common[None], (owner_count,) + common.shape)
    codes = jnp.pad(
        codes[:, None, :],
        ((0, 0), (ROWS // 2, 15), (2 * CIRCLE_USERS, 2 * H - 2 * CIRCLE_USERS - 2 * CAP)),
    )
    arrived = lax.all_to_all(sent + codes, "shard", split_axis=0, concat_axis=0, tiled=True)
    asked = arrived[:, ROWS // 2, 2 * CIRCLE_USERS : 2 * CIRCLE_USERS + 2 * CAP].astype(jnp.int32)

    vt = tower_vectors(item_features, tower_weight.T)
    gates = (gate_in, gate_in_bias[None, :], gate_out, gate_out_bias[None, :])
    keep, send = pair_terms(asked, group[None], arrived, vt, item_features, gates)
    terms = (keep + swapped(send, 1).astype(F32)).astype(BF)
    terms = lax.all_to_all(terms, "shard", split_axis=0, concat_axis=0, tiled=True)
    sums = jnp.sum(terms.astype(F32), axis=0)
    rows = sums.shape[0] - K
    half = sums[:rows]
    from_1, from_2, from_3 = swapped(half, 1), swapped(sums, 2), swapped(half, 3)
    mine = half + from_2[:rows]
    other = from_1 + from_3
    even = group % 2 == 0
    tower_gradient = jnp.concatenate(
        [jnp.where(even, mine, other), jnp.where(even, other, mine)], axis=0
    )
    user_delta = sums[rows:, : USERS * H] + from_2[rows:, USERS * H :]
    user_delta = user_delta.reshape(K, USERS, H).transpose(1, 0, 2).reshape(USERS, E)
    user_gradient = split_product(row_match.astype(BF), user_delta)
    return (tower_gradient, user_gradient)


def solution(mesh):
    return jax.shard_map(
        shards,
        mesh=mesh,
        in_specs=(
            P("shard", None),
            P(),
            P(),
            P(),
            P(),
            P(),
            P(("blk", "shard"), None),
            P(("blk", "shard")),
            P(("blk", "shard"), None),
            P(("blk", "shard"), None),
            P(("blk", "shard")),
        ),
        out_specs=(P("shard", None), P(("blk", "shard"), None)),
        check_vma=False,
    )
```

```python
import math

import jax
import jax.numpy as jnp
from jax import lax
from jax.experimental import pallas as pl
from jax.experimental.pallas import tpu as pltpu
from jax.sharding import PartitionSpec as P

K = 8
H = 64
BLK = 128
CAP = 2
OWN = 32
STAY = 16
MOVE = 4
MOST = 5 * CAP
SIDE = 4
USERS = 4
TILE_USERS = 2
UTAB = 128
E = 512
GROUPS = 4
CIRCLE_USERS = GROUPS * USERS
ROWS = CIRCLE_USERS * K
PAIRS = K * K
F32 = jnp.float32
BF = jnp.bfloat16
VMEM_SPEC = pl.BlockSpec(memory_space=pltpu.VMEM)


def swapped(x, by):
    return lax.ppermute(x, "blk", [(i, i ^ by) for i in range(GROUPS)])


NEIGHBOURS = ((1, 1), (1, -1), (SIDE, 1), (SIDE, -1))


def neighbour(shard, stride, by):
    digit = shard // stride % SIDE
    return shard + ((digit + by) % SIDE - digit) * stride


def along(x, devices, stride, by):
    pairs = [(i, neighbour(i, stride, by)) for i in range(devices)]
    return lax.ppermute(x, "shard", pairs)


def serving_device(owner, slot):
    device = owner
    for i, (stride, by) in enumerate(NEIGHBOURS):
        here = jnp.logical_and(slot >= STAY + i * MOVE, slot < STAY + (i + 1) * MOVE)
        device = jnp.where(here, neighbour(owner, stride, by), device)
    return device


def tower_kernel(weight, *refs):
    out = refs[-1]
    blocks = out.shape[0] // (len(refs) - 1)
    for part, features in enumerate(refs[:-1]):
        product = jnp.dot(features[...], weight[...], preferred_element_type=F32).astype(BF)
        for c in range(blocks):
            turned = product[c * BLK : (c + 1) * BLK, :].T
            for b in range(K):
                out[part * blocks + c, :, b * BLK : (b + 1) * BLK] = turned[
                    b * H : (b + 1) * H, :
                ]


def tower_vectors(weight, stay, parts):
    width = weight.shape[0]
    if stay is not None:
        blocks = 8
        grid = (STAY // blocks,)
        operands = [stay]
        specs = [pl.BlockSpec((blocks * BLK, width), lambda i: (i, 0))]
    else:
        blocks = MOVE * len(parts)
        grid = (1,)
        operands = parts
        specs = [pl.BlockSpec((MOVE * BLK, width), lambda i: (0, 0))] * len(parts)
    total = blocks * grid[0]
    return pl.pallas_call(
        tower_kernel,
        grid=grid,
        in_specs=[pl.BlockSpec((width, E), lambda i: (0, 0))] + specs,
        out_specs=pl.BlockSpec((blocks, H, K * BLK), lambda i: (i, 0, 0)),
        out_shape=jax.ShapeDtypeStruct((total, H, K * BLK), BF),
        compiler_params=pltpu.CompilerParams(vmem_limit_bytes=58 << 20),
        cost_estimate=pl.CostEstimate(
            flops=2 * total * BLK * E * width, bytes_accessed=7 << 20, transcendentals=0
        ),
        name="tower_stay" if stay is not None else "tower_moved",
    )(weight, *operands)


def pair_kernel(codes, group, arrived_any, vt_stay, vt_moved, features_stay, moved_0, moved_1,
                moved_2, moved_3, gate_in, gate_in_bias, gate_out_t, gate_out_bias, keep, send, first_half, first, second_t, second_half,
                bias1, bias2, arrived, vt, features, grads, deltas, total,
                entry_slot, entry_shard, entry_start, sems, *buffers):
    step_rows = MOVE * BLK
    pieces = [
        (arrived_any, arrived),
        (vt_stay, vt.at[pl.ds(0, STAY)]),
        (vt_moved, vt.at[pl.ds(STAY, OWN - STAY)]),
        (features_stay.at[pl.ds(0, STAY * BLK), :], features.at[pl.ds(0, STAY * BLK), :]),
    ] + [
        (part, features.at[pl.ds(STAY * BLK + i * step_rows, step_rows), :])
        for i, part in enumerate((moved_0, moved_1, moved_2, moved_3))
    ]
    copies = [
        pltpu.make_async_copy(source, target, sems.at[i])
        for i, (source, target) in enumerate(pieces)
    ]
    for copy in copies[:3]:
        copy.start()
    owners = codes.shape[0]
    logits, hidden, slope, weights, back, pair_grad = [
        buffers[2 * i : 2 * i + 2] for i in range(6)
    ]
    tile = TILE_USERS * BLK
    tiles = CIRCLE_USERS // TILE_USERS

    def idle(position):
        entry_slot[position] = OWN
        entry_shard[position] = owners
        entry_start[position] = 0

    def enter_shard(shard, count):
        def enter(rank, position):
            entry_slot[position + 2] = codes[shard, 1 + rank]
            entry_shard[position + 2] = shard
            entry_start[position + 2] = codes[shard, 1 + MOST + rank] * BLK
            return position + 1

        return lax.fori_loop(0, jnp.minimum(codes[shard, 0], MOST), enter, count)

    count = lax.fori_loop(0, owners, enter_shard, 0)
    for position in (0, 1, count + 2, count + 3, count + 4):
        idle(position)
    grads[...] = jnp.zeros_like(grads)
    deltas[...] = jnp.zeros_like(deltas)
    lane = lax.broadcasted_iota(jnp.int32, (16, BLK), 1).astype(F32)
    row = lax.broadcasted_iota(jnp.int32, (PAIRS, PAIRS), 0)
    column = lax.broadcasted_iota(jnp.int32, (PAIRS, PAIRS), 1)
    order = jnp.where(column == (row & (K - 1)) * K + (row >> 3), 1.0, 0.0).astype(BF)
    across = (((1,), (1,)), ((), ()))
    turned_in = jnp.dot(order, gate_in[...], preferred_element_type=F32)
    turned_out = jnp.dot(order, gate_out_t[...], preferred_element_type=F32)
    first[...] = turned_in.astype(BF)
    first_half[...] = (turned_in.T * 0.5).astype(BF)
    second_t[...] = turned_out.astype(BF)
    second_half[...] = (turned_out.T * 0.5).astype(BF)
    bias1[...] = jnp.broadcast_to(gate_in_bias[...].astype(F32) * 0.5, bias1.shape).T
    bias2[...] = lax.dot_general(
        order,
        jnp.broadcast_to(gate_out_bias[...], (BLK, PAIRS)),
        across,
        preferred_element_type=F32,
    )
    for copy in copies[:3]:
        copy.wait()
    for copy in copies[3:]:
        copy.start()

    def users_of(shard):
        packed = arrived[jnp.minimum(shard, owners - 1), 0 : ROWS // 2, :]
        return jnp.concatenate([packed[:, :H], packed[:, H:]], axis=0)

    def items_of(slot):
        return vt[jnp.minimum(slot, OWN - 1)]

    def logits_of(ref, k):
        return jnp.concatenate(
            [
                jnp.concatenate(
                    [ref[u * K : (u + 1) * K, b * BLK : (b + 1) * BLK] for b in range(K)],
                    axis=0,
                )
                for u in range(TILE_USERS * k, TILE_USERS * (k + 1))
            ],
            axis=1,
        )

    def stages(n, even):
        odd = 1 - even
        start_slot, start_shard = entry_slot[n + 2], entry_shard[n + 2]
        middle_shard, middle_start = entry_shard[n + 1], entry_start[n + 1]
        end_slot, end_shard = entry_slot[n], entry_shard[n]
        meta = arrived[jnp.minimum(middle_shard, owners - 1), ROWS // 2 : ROWS // 2 + 16, :]
        meta = meta.astype(F32)
        offset = meta[:, 0:16] * BLK + meta[:, 16:32] - middle_start.astype(F32)

        def scores():
            logits[even][...] = jnp.dot(
                users_of(start_shard), items_of(start_slot), preferred_element_type=F32
            )

        def forward(k):
            columns = slice(k * tile, (k + 1) * tile)
            h = jnp.dot(
                first_half[...],
                logits_of(logits[even], k).astype(BF),
                preferred_element_type=F32,
            ) + jnp.concatenate([bias1[...]] * TILE_USERS, axis=1)
            t = jnp.tanh(h)
            q = 1.0 + t
            silu = h * q
            hidden[even][:, columns] = silu.astype(BF)
            slope[even][:, columns] = q + silu * (1.0 - t)

        def mix(k):
            columns = slice(k * tile, (k + 1) * tile)
            users = range(TILE_USERS * k, TILE_USERS * (k + 1))
            y = jnp.concatenate(
                [
                    jnp.max(
                        jnp.where(offset[:, u : u + 1] == lane, 1.0, 0.0), axis=0, keepdims=True
                    )
                    for u in users
                ],
                axis=1,
            )
            gate = jnp.dot(
                second_t[...], hidden[odd][:, columns], preferred_element_type=F32
            ) + jnp.concatenate([bias2[...]] * TILE_USERS, axis=1)
            e = jnp.exp(gate)
            lk = logits_of(logits[odd], k)
            inverse = 1.0 / jnp.sum(e, axis=0, keepdims=True)
            score = jnp.sum(e * lk, axis=0, keepdims=True) * inverse
            score_grad = 0.5 + 0.5 * jnp.tanh(0.5 * score) - y
            weighted = e * (score_grad * inverse)
            weights[odd][:, columns] = weighted
            return (weighted * (lk - score)).astype(BF)

        def gate_back(k, logit_grad):
            columns = slice(k * tile, (k + 1) * tile)
            hidden_grad = jnp.dot(second_half[...], logit_grad, preferred_element_type=F32)
            back[odd][:, columns] = (hidden_grad * slope[odd][:, columns]).astype(BF)

        def pair_back(k):
            columns = slice(k * tile, (k + 1) * tile)
            pg = jnp.dot(first[...], back[even][:, columns], preferred_element_type=F32)
            pg = pg + weights[even][:, columns]
            rows = slice(K * TILE_USERS * k, K * TILE_USERS * (k + 1))
            for b in range(K):
                pair_grad[even][rows, b * BLK : (b + 1) * BLK] = jnp.concatenate(
                    [
                        pg[b * K : (b + 1) * K, w * BLK : (w + 1) * BLK]
                        for w in range(TILE_USERS)
                    ],
                    axis=0,
                ).astype(BF)

        for k in range(tiles):
            pair_back(k)
        scores()
        logit_grads = [mix(k) for k in range(tiles)]
        pgv = pair_grad[even][...]
        deltas[end_shard] += lax.dot_general(
            pgv, items_of(end_slot), (((1,), (1,)), ((), ())), preferred_element_type=F32
        )
        grads[end_slot] += jnp.dot(users_of(end_shard).T, pgv, preferred_element_type=F32)
        for k in range(tiles):
            forward(k)
            gate_back(k, logit_grads[k])

    def step(i, carry):
        stages(2 * i, 0)
        stages(2 * i + 1, 1)
        return carry

    lax.fori_loop(0, (count + 3) // 2, step, 0)

    rows = keep.shape[1] - K
    scaling = 1.0 / math.sqrt(H)
    piece = USERS * K
    for c in range(2 * USERS):
        columns = slice(c * H, (c + 1) * H)
        first_row = 2 * piece * (c // USERS) + K * (c % USERS)
        keep[:, rows:, columns] = deltas[0:owners, first_row : first_row + K, :] * scaling
        first_row = first_row + piece
        send[:, rows:, columns] = (
            deltas[0:owners, first_row : first_row + K, :] * scaling
        ).astype(BF)
    for copy in copies[3:]:
        copy.wait()
    blocks = 8

    def add(i, carry):
        left = jnp.concatenate(
            [
                jnp.concatenate(
                    [
                        grads[i * blocks + c, :, b * BLK : (b + 1) * BLK].astype(BF)
                        for b in range(K)
                    ],
                    axis=0,
                )
                for c in range(blocks)
            ],
            axis=1,
        )
        start = pl.multiple_of(i * blocks * BLK, blocks * BLK)
        product = jnp.dot(
            left, features[pl.ds(start, blocks * BLK), :], preferred_element_type=F32
        )

        @pl.when(i == 0)
        def _():
            total[...] = product

        @pl.when(i > 0)
        def _():
            total[...] += product

        return carry

    lax.fori_loop(0, OWN // blocks, add, 0)
    parity = group[0] & 1
    for part in range(total.shape[1] // BLK):
        turned = total[:, part * BLK : (part + 1) * BLK].T
        for c in range(BLK // (2 * rows)):
            lower = turned[2 * rows * c : 2 * rows * c + rows, :]
            upper = turned[2 * rows * c + rows : 2 * rows * (c + 1), :]
            owner = part * (BLK // (2 * rows)) + c
            keep[owner, 0:rows, :] = jnp.where(parity == 0, lower, upper)
            send[owner, 0:rows, :] = jnp.where(parity == 0, upper, lower).astype(BF)


def pair_terms(codes, group, arrived, vectors, features, gates):
    owners = codes.shape[0]
    width = features[0].shape[1]
    any_spec = pl.BlockSpec(memory_space=pl.ANY)
    columns = CIRCLE_USERS * BLK
    hidden = gates[0].shape[1]
    shape = (owners, width // (2 * owners) + K, E)
    smem = pl.BlockSpec(memory_space=pltpu.SMEM)

    def twice(shape, dtype):
        return [pltpu.VMEM(shape, dtype)] * 2

    return pl.pallas_call(
        pair_kernel,
        out_shape=(jax.ShapeDtypeStruct(shape, F32), jax.ShapeDtypeStruct(shape, BF)),
        in_specs=[smem] * 2 + [any_spec] * 8 + [VMEM_SPEC] * 4,
        out_specs=(VMEM_SPEC, VMEM_SPEC),
        scratch_shapes=[
            pltpu.VMEM((hidden, PAIRS), BF),
            pltpu.VMEM((PAIRS, hidden), BF),
            pltpu.VMEM((PAIRS, hidden), BF),
            pltpu.VMEM((hidden, PAIRS), BF),
            pltpu.VMEM((hidden, BLK), F32),
            pltpu.VMEM((PAIRS, BLK), F32),
            pltpu.VMEM(arrived.shape, BF),
            pltpu.VMEM((OWN, H, K * BLK), BF),
            pltpu.VMEM((OWN * BLK, width), BF),
            pltpu.VMEM((OWN + 1, H, K * BLK), F32),
            pltpu.VMEM((owners + 1, ROWS, H), F32),
            pltpu.VMEM((E, width), F32),
            pltpu.SMEM((owners * MOST + 8,), jnp.int32),
            pltpu.SMEM((owners * MOST + 8,), jnp.int32),
            pltpu.SMEM((owners * MOST + 8,), jnp.int32),
            pltpu.SemaphoreType.DMA((8,)),
        ]
        + twice((ROWS, K * BLK), F32)
        + twice((hidden, columns), BF)
        + twice((hidden, columns), F32)
        + twice((PAIRS, columns), F32)
        + twice((hidden, columns), BF)
        + twice((ROWS, K * BLK), BF),
        compiler_params=pltpu.CompilerParams(vmem_limit_bytes=58 << 20),
        cost_estimate=pl.CostEstimate(
            flops=40 << 30, bytes_accessed=16 << 20, transcendentals=1 << 24
        ),
        name="pairs",
    )(codes, group, arrived, *vectors, *features, *gates)


def split_product(left_bf16, right_f32):
    upper = right_f32.astype(BF)
    lower = (right_f32 - upper.astype(F32)).astype(BF)
    dims = (((0,), (0,)), ((), ()))
    first = lax.dot_general(left_bf16, upper, dims, preferred_element_type=F32)
    second = lax.dot_general(left_bf16, lower, dims, preferred_element_type=F32)
    return first + second


def shards(
    item_features,
    tower_weight,
    gate_in,
    gate_in_bias,
    gate_out,
    gate_out_bias,
    user_table,
    user_ids,
    positive_item,
    listed_owner,
    listed_slot,
):
    owner_count = lax.axis_size("shard")
    group = lax.axis_index("blk")
    moved = [
        along(
            item_features[(STAY + i * MOVE) * BLK : (STAY + (i + 1) * MOVE) * BLK],
            owner_count,
            stride,
            by,
        )
        for i, (stride, by) in enumerate(NEIGHBOURS)
    ]
    listings = listed_slot.shape[0]
    owner_ids = listed_owner[:, 0]
    served_by = serving_device(owner_ids, listed_slot)
    order = jnp.arange(listings, dtype=jnp.int32)
    same_device = served_by[:, None] == served_by[None, :]
    earlier = order[None, :] < order[:, None]
    rank_within = jnp.sum(jnp.logical_and(same_device, earlier), axis=1)
    device_match = served_by[:, None] == jnp.arange(owner_count, dtype=jnp.int32)[None, :]
    place = group * listings + order
    column = jnp.arange(1 + 2 * MOST, dtype=jnp.int32)[None, :]
    value = jnp.where(
        column == 0,
        1,
        jnp.where(column == 1 + rank_within[:, None], listed_slot[:, None], 0)
        + jnp.where(column == 1 + MOST + rank_within[:, None], place[:, None], 0),
    )
    codes = jnp.sum(
        jnp.where(device_match[:, :, None], value[:, None, :], 0), axis=0
    ).astype(BF)

    row_match = user_ids[:, None] == jnp.arange(UTAB, dtype=jnp.int32)[None, :]
    user_rows = jnp.dot(row_match.astype(BF), user_table, preferred_element_type=F32)
    user_rows = (user_rows * (1.0 / math.sqrt(H))).astype(BF).reshape(USERS * K, H)
    positives = positive_item.T
    marks = jnp.concatenate([positives // BLK, positives % BLK], axis=1).astype(BF)
    own = jnp.concatenate([user_rows, jnp.pad(marks, ((0, 0), (0, H - 2 * USERS)))], axis=0)
    pieces = [own] + [swapped(own, by) for by in range(1, GROUPS)]
    rows = [piece[: USERS * K] for piece in pieces]
    marks = [piece[USERS * K :] for piece in pieces]
    packed = jnp.concatenate(
        [jnp.concatenate(rows[0:2], axis=0), jnp.concatenate(rows[2:4], axis=0)], axis=1
    )
    meta = jnp.concatenate(
        [m[:, :USERS] for m in marks] + [m[:, USERS : 2 * USERS] for m in marks], axis=1
    )
    meta = jnp.pad(meta, ((0, 0), (0, 2 * H - 2 * CIRCLE_USERS)))
    common = jnp.concatenate([packed, meta], axis=0)
    sent = jnp.broadcast_to(common[None], (owner_count,) + common.shape)
    codes = jnp.pad(
        codes[:, None, :],
        ((0, 0), (ROWS // 2, 15), (2 * CIRCLE_USERS, 2 * H - 2 * CIRCLE_USERS - 1 - 2 * MOST)),
    )
    arrived = lax.all_to_all(sent + codes, "shard", split_axis=0, concat_axis=0, tiled=True)
    asked = arrived[:, ROWS // 2, 2 * CIRCLE_USERS : 2 * CIRCLE_USERS + 1 + 2 * MOST].astype(jnp.int32)

    vectors = (
        tower_vectors(tower_weight, item_features, None),
        tower_vectors(tower_weight, None, moved),
    )
    gates = (gate_in, gate_in_bias[None, :], gate_out.T, gate_out_bias[None, :])
    keep, send = pair_terms(
        asked, group[None], arrived, vectors, (item_features, *moved), gates
    )
    terms = (keep + swapped(send, 1).astype(F32)).astype(BF)
    terms = lax.all_to_all(terms, "shard", split_axis=0, concat_axis=0, tiled=True)
    sums = jnp.sum(terms.astype(F32), axis=0)
    rows = sums.shape[0] - K
    half = sums[:rows]
    from_1, from_2, from_3 = swapped(half, 1), swapped(sums, 2), swapped(half, 3)
    mine = half + from_2[:rows]
    other = from_1 + from_3
    even = group % 2 == 0
    tower_gradient = jnp.concatenate(
        [jnp.where(even, mine, other), jnp.where(even, other, mine)], axis=0
    )
    user_delta = sums[rows:, : USERS * H] + from_2[rows:, USERS * H :]
    user_delta = user_delta.reshape(K, USERS, H).transpose(1, 0, 2).reshape(USERS, E)
    user_gradient = split_product(row_match.astype(BF), user_delta)
    return (tower_gradient, user_gradient)


def solution(mesh):
    return jax.shard_map(
        shards,
        mesh=mesh,
        in_specs=(
            P("shard", None),
            P(),
            P(),
            P(),
            P(),
            P(),
            P(("blk", "shard"), None),
            P(("blk", "shard")),
            P(("blk", "shard"), None),
            P(("blk", "shard"), None),
            P(("blk", "shard")),
        ),
        out_specs=(P("shard", None), P(("blk", "shard"), None)),
        check_vma=False,
    )
```

```python
import math

import jax
import jax.numpy as jnp
from jax import lax
from jax.experimental import pallas as pl
from jax.experimental.pallas import tpu as pltpu
from jax.sharding import PartitionSpec as P

K = 8
H = 64
BLK = 128
CAP = 2
OWN = 32
STAY = 16
MOVE = 4
HALF = MOVE // 2
MOST = 5 * CAP
SIDE = 4
USERS = 4
TILE_USERS = 2
UTAB = 128
E = 512
GROUPS = 4
CIRCLE_USERS = GROUPS * USERS
ROWS = CIRCLE_USERS * K
PAIRS = K * K
F32 = jnp.float32
BF = jnp.bfloat16
VMEM_SPEC = pl.BlockSpec(memory_space=pltpu.VMEM)


def swapped(x, by):
    return lax.ppermute(x, "blk", [(i, i ^ by) for i in range(GROUPS)])


NEIGHBOURS = ((1, 1), (1, -1), (SIDE, 1), (SIDE, -1))


def neighbour(shard, stride, by):
    digit = shard // stride % SIDE
    return shard + ((digit + by) % SIDE - digit) * stride


def along(x, devices, stride, by):
    pairs = [(i, neighbour(i, stride, by)) for i in range(devices)]
    return lax.ppermute(x, "shard", pairs)


def serving_device(owner, slot):
    device = owner
    for i, (stride, by) in enumerate(NEIGHBOURS):
        here = jnp.logical_and(slot >= STAY + i * MOVE, slot < STAY + (i + 1) * MOVE)
        device = jnp.where(here, neighbour(owner, stride, by), device)
    return device


def tower_kernel(weight, *refs):
    out = refs[-1]
    blocks = out.shape[0] // (len(refs) - 1)
    for part, features in enumerate(refs[:-1]):
        product = jnp.dot(features[...], weight[...], preferred_element_type=F32).astype(BF)
        for c in range(blocks):
            turned = product[c * BLK : (c + 1) * BLK, :].T
            for b in range(K):
                out[part * blocks + c, :, b * BLK : (b + 1) * BLK] = turned[
                    b * H : (b + 1) * H, :
                ]


def tower_vectors(weight, stay, parts):
    width = weight.shape[0]
    if stay is not None:
        blocks = 8
        grid = (STAY // blocks,)
        operands = [stay]
        specs = [pl.BlockSpec((blocks * BLK, width), lambda i: (i, 0))]
    else:
        blocks = HALF * len(parts)
        grid = (1,)
        operands = parts
        specs = [pl.BlockSpec((HALF * BLK, width), lambda i: (0, 0))] * len(parts)
    total = blocks * grid[0]
    return pl.pallas_call(
        tower_kernel,
        grid=grid,
        in_specs=[pl.BlockSpec((width, E), lambda i: (0, 0))] + specs,
        out_specs=pl.BlockSpec((blocks, H, K * BLK), lambda i: (i, 0, 0)),
        out_shape=jax.ShapeDtypeStruct((total, H, K * BLK), BF),
        compiler_params=pltpu.CompilerParams(vmem_limit_bytes=58 << 20),
        cost_estimate=pl.CostEstimate(
            flops=2 * total * BLK * E * width, bytes_accessed=7 << 20, transcendentals=0
        ),
        name="tower_stay" if stay is not None else "tower_moved",
    )(weight, *operands)


def pair_kernel(codes, group, arrived_any, vt_stay, vt_moved, features_stay, moved_0, moved_1,
                moved_2, moved_3, moved_4, moved_5, moved_6, moved_7, gate_in, gate_in_bias, gate_out_t, gate_out_bias, keep, send, first_half, first, second_t, second_half,
                bias1, bias2, arrived, vt, features, grads, deltas, total,
                entry_slot, entry_shard, entry_start, sems, *buffers):
    step_rows = HALF * BLK
    moved = (moved_0, moved_1, moved_2, moved_3, moved_4, moved_5, moved_6, moved_7)
    pieces = [
        (arrived_any, arrived),
        (vt_stay, vt.at[pl.ds(0, STAY)]),
        (vt_moved, vt.at[pl.ds(STAY, OWN - STAY)]),
        (features_stay.at[pl.ds(0, STAY * BLK), :], features.at[pl.ds(0, STAY * BLK), :]),
    ] + [
        (part, features.at[pl.ds(STAY * BLK + i * step_rows, step_rows), :])
        for i, part in enumerate(moved)
    ]
    copies = [
        pltpu.make_async_copy(source, target, sems.at[i])
        for i, (source, target) in enumerate(pieces)
    ]
    for copy in copies[:3]:
        copy.start()
    owners = codes.shape[0]
    logits, hidden, slope, weights, back, pair_grad = [
        buffers[2 * i : 2 * i + 2] for i in range(6)
    ]
    tile = TILE_USERS * BLK
    tiles = CIRCLE_USERS // TILE_USERS

    def idle(position):
        entry_slot[position] = OWN
        entry_shard[position] = owners
        entry_start[position] = 0

    def enter_shard(shard, count):
        def enter(rank, position):
            slot = codes[shard, 1 + rank]
            upper = jnp.maximum(slot - STAY, 0) // HALF % 2
            turn = jnp.where(upper == 0, HALF, -HALF) * (group[0] & 1)
            entry_slot[position + 2] = slot + jnp.where(slot >= STAY, turn, 0)
            entry_shard[position + 2] = shard
            entry_start[position + 2] = codes[shard, 1 + MOST + rank] * BLK
            return position + 1

        return lax.fori_loop(0, jnp.minimum(codes[shard, 0], MOST), enter, count)

    count = lax.fori_loop(0, owners, enter_shard, 0)
    for position in (0, 1, count + 2, count + 3, count + 4):
        idle(position)
    grads[...] = jnp.zeros_like(grads)
    deltas[...] = jnp.zeros_like(deltas)
    lane = lax.broadcasted_iota(jnp.int32, (16, BLK), 1).astype(F32)
    row = lax.broadcasted_iota(jnp.int32, (PAIRS, PAIRS), 0)
    column = lax.broadcasted_iota(jnp.int32, (PAIRS, PAIRS), 1)
    order = jnp.where(column == (row & (K - 1)) * K + (row >> 3), 1.0, 0.0).astype(BF)
    across = (((1,), (1,)), ((), ()))
    turned_in = jnp.dot(order, gate_in[...], preferred_element_type=F32)
    turned_out = jnp.dot(order, gate_out_t[...], preferred_element_type=F32)
    first[...] = turned_in.astype(BF)
    first_half[...] = (turned_in.T * 0.5).astype(BF)
    second_t[...] = turned_out.astype(BF)
    second_half[...] = (turned_out.T * 0.5).astype(BF)
    bias1[...] = jnp.broadcast_to(gate_in_bias[...].astype(F32) * 0.5, bias1.shape).T
    bias2[...] = lax.dot_general(
        order,
        jnp.broadcast_to(gate_out_bias[...], (BLK, PAIRS)),
        across,
        preferred_element_type=F32,
    )
    for copy in copies[:3]:
        copy.wait()
    for copy in copies[3:]:
        copy.start()

    def users_of(shard):
        packed = arrived[jnp.minimum(shard, owners - 1), 0 : ROWS // 2, :]
        return jnp.concatenate([packed[:, :H], packed[:, H:]], axis=0)

    def items_of(slot):
        return vt[jnp.minimum(slot, OWN - 1)]

    def logits_of(ref, k):
        return jnp.concatenate(
            [
                jnp.concatenate(
                    [ref[u * K : (u + 1) * K, b * BLK : (b + 1) * BLK] for b in range(K)],
                    axis=0,
                )
                for u in range(TILE_USERS * k, TILE_USERS * (k + 1))
            ],
            axis=1,
        )

    def stages(n, even):
        odd = 1 - even
        start_slot, start_shard = entry_slot[n + 2], entry_shard[n + 2]
        middle_shard, middle_start = entry_shard[n + 1], entry_start[n + 1]
        end_slot, end_shard = entry_slot[n], entry_shard[n]
        meta = arrived[jnp.minimum(middle_shard, owners - 1), ROWS // 2 : ROWS // 2 + 16, :]
        meta = meta.astype(F32)
        offset = meta[:, 0:16] * BLK + meta[:, 16:32] - middle_start.astype(F32)

        def scores():
            logits[even][...] = jnp.dot(
                users_of(start_shard), items_of(start_slot), preferred_element_type=F32
            )

        def forward(k):
            columns = slice(k * tile, (k + 1) * tile)
            h = jnp.dot(
                first_half[...],
                logits_of(logits[even], k).astype(BF),
                preferred_element_type=F32,
            ) + jnp.concatenate([bias1[...]] * TILE_USERS, axis=1)
            t = jnp.tanh(h)
            q = 1.0 + t
            silu = h * q
            hidden[even][:, columns] = silu.astype(BF)
            slope[even][:, columns] = q + silu * (1.0 - t)

        def mix(k):
            columns = slice(k * tile, (k + 1) * tile)
            users = range(TILE_USERS * k, TILE_USERS * (k + 1))
            y = jnp.concatenate(
                [
                    jnp.max(
                        jnp.where(offset[:, u : u + 1] == lane, 1.0, 0.0), axis=0, keepdims=True
                    )
                    for u in users
                ],
                axis=1,
            )
            gate = jnp.dot(
                second_t[...], hidden[odd][:, columns], preferred_element_type=F32
            ) + jnp.concatenate([bias2[...]] * TILE_USERS, axis=1)
            e = jnp.exp(gate)
            lk = logits_of(logits[odd], k)
            inverse = 1.0 / jnp.sum(e, axis=0, keepdims=True)
            score = jnp.sum(e * lk, axis=0, keepdims=True) * inverse
            score_grad = 0.5 + 0.5 * jnp.tanh(0.5 * score) - y
            weighted = e * (score_grad * inverse)
            weights[odd][:, columns] = weighted
            return (weighted * (lk - score)).astype(BF)

        def gate_back(k, logit_grad):
            columns = slice(k * tile, (k + 1) * tile)
            hidden_grad = jnp.dot(second_half[...], logit_grad, preferred_element_type=F32)
            back[odd][:, columns] = (hidden_grad * slope[odd][:, columns]).astype(BF)

        def pair_back(k):
            columns = slice(k * tile, (k + 1) * tile)
            pg = jnp.dot(first[...], back[even][:, columns], preferred_element_type=F32)
            pg = pg + weights[even][:, columns]
            rows = slice(K * TILE_USERS * k, K * TILE_USERS * (k + 1))
            for b in range(K):
                pair_grad[even][rows, b * BLK : (b + 1) * BLK] = jnp.concatenate(
                    [
                        pg[b * K : (b + 1) * K, w * BLK : (w + 1) * BLK]
                        for w in range(TILE_USERS)
                    ],
                    axis=0,
                ).astype(BF)

        for k in range(tiles):
            pair_back(k)
        scores()
        logit_grads = [mix(k) for k in range(tiles)]
        pgv = pair_grad[even][...]
        deltas[end_shard] += lax.dot_general(
            pgv, items_of(end_slot), (((1,), (1,)), ((), ())), preferred_element_type=F32
        )
        grads[end_slot] += jnp.dot(users_of(end_shard).T, pgv, preferred_element_type=F32)
        for k in range(tiles):
            forward(k)
            gate_back(k, logit_grads[k])

    def step(i, carry):
        stages(2 * i, 0)
        stages(2 * i + 1, 1)
        return carry

    lax.fori_loop(0, (count + 3) // 2, step, 0)

    rows = keep.shape[1] - K
    scaling = 1.0 / math.sqrt(H)
    piece = USERS * K
    for c in range(2 * USERS):
        columns = slice(c * H, (c + 1) * H)
        first_row = 2 * piece * (c // USERS) + K * (c % USERS)
        keep[:, rows:, columns] = deltas[0:owners, first_row : first_row + K, :] * scaling
        first_row = first_row + piece
        send[:, rows:, columns] = (
            deltas[0:owners, first_row : first_row + K, :] * scaling
        ).astype(BF)
    for copy in copies[3:]:
        copy.wait()
    blocks = 8

    def add(i, carry):
        left = jnp.concatenate(
            [
                jnp.concatenate(
                    [
                        grads[i * blocks + c, :, b * BLK : (b + 1) * BLK].astype(BF)
                        for b in range(K)
                    ],
                    axis=0,
                )
                for c in range(blocks)
            ],
            axis=1,
        )
        start = pl.multiple_of(i * blocks * BLK, blocks * BLK)
        product = jnp.dot(
            left, features[pl.ds(start, blocks * BLK), :], preferred_element_type=F32
        )

        @pl.when(i == 0)
        def _():
            total[...] = product

        @pl.when(i > 0)
        def _():
            total[...] += product

        return carry

    lax.fori_loop(0, OWN // blocks, add, 0)
    parity = group[0] & 1
    for part in range(total.shape[1] // BLK):
        turned = total[:, part * BLK : (part + 1) * BLK].T
        for c in range(BLK // (2 * rows)):
            lower = turned[2 * rows * c : 2 * rows * c + rows, :]
            upper = turned[2 * rows * c + rows : 2 * rows * (c + 1), :]
            owner = part * (BLK // (2 * rows)) + c
            keep[owner, 0:rows, :] = jnp.where(parity == 0, lower, upper)
            send[owner, 0:rows, :] = jnp.where(parity == 0, upper, lower).astype(BF)


def pair_terms(codes, group, arrived, vectors, features, gates):
    owners = codes.shape[0]
    width = features[0].shape[1]
    any_spec = pl.BlockSpec(memory_space=pl.ANY)
    columns = CIRCLE_USERS * BLK
    hidden = gates[0].shape[1]
    shape = (owners, width // (2 * owners) + K, E)
    smem = pl.BlockSpec(memory_space=pltpu.SMEM)

    def twice(shape, dtype):
        return [pltpu.VMEM(shape, dtype)] * 2

    return pl.pallas_call(
        pair_kernel,
        out_shape=(jax.ShapeDtypeStruct(shape, F32), jax.ShapeDtypeStruct(shape, BF)),
        in_specs=[smem] * 2 + [any_spec] * 12 + [VMEM_SPEC] * 4,
        out_specs=(VMEM_SPEC, VMEM_SPEC),
        scratch_shapes=[
            pltpu.VMEM((hidden, PAIRS), BF),
            pltpu.VMEM((PAIRS, hidden), BF),
            pltpu.VMEM((PAIRS, hidden), BF),
            pltpu.VMEM((hidden, PAIRS), BF),
            pltpu.VMEM((hidden, BLK), F32),
            pltpu.VMEM((PAIRS, BLK), F32),
            pltpu.VMEM(arrived.shape, BF),
            pltpu.VMEM((OWN, H, K * BLK), BF),
            pltpu.VMEM((OWN * BLK, width), BF),
            pltpu.VMEM((OWN + 1, H, K * BLK), F32),
            pltpu.VMEM((owners + 1, ROWS, H), F32),
            pltpu.VMEM((E, width), F32),
            pltpu.SMEM((owners * MOST + 8,), jnp.int32),
            pltpu.SMEM((owners * MOST + 8,), jnp.int32),
            pltpu.SMEM((owners * MOST + 8,), jnp.int32),
            pltpu.SemaphoreType.DMA((12,)),
        ]
        + twice((ROWS, K * BLK), F32)
        + twice((hidden, columns), BF)
        + twice((hidden, columns), F32)
        + twice((PAIRS, columns), F32)
        + twice((hidden, columns), BF)
        + twice((ROWS, K * BLK), BF),
        compiler_params=pltpu.CompilerParams(vmem_limit_bytes=58 << 20),
        cost_estimate=pl.CostEstimate(
            flops=40 << 30, bytes_accessed=16 << 20, transcendentals=1 << 24
        ),
        name="pairs",
    )(codes, group, arrived, *vectors, *features, *gates)


def split_product(left_bf16, right_f32):
    upper = right_f32.astype(BF)
    lower = (right_f32 - upper.astype(F32)).astype(BF)
    dims = (((0,), (0,)), ((), ()))
    first = lax.dot_general(left_bf16, upper, dims, preferred_element_type=F32)
    second = lax.dot_general(left_bf16, lower, dims, preferred_element_type=F32)
    return first + second


def shards(
    item_features,
    tower_weight,
    gate_in,
    gate_in_bias,
    gate_out,
    gate_out_bias,
    user_table,
    user_ids,
    positive_item,
    listed_owner,
    listed_slot,
):
    owner_count = lax.axis_size("shard")
    group = lax.axis_index("blk")
    halves = []
    for i, (stride, by) in enumerate(NEIGHBOURS):
        first = (STAY + i * MOVE + group % 2 * HALF) * BLK
        half = lax.dynamic_slice_in_dim(item_features, first, HALF * BLK, axis=0)
        halves.append(along(half, owner_count, stride, by))
    halves, tower_weight = lax.optimization_barrier((halves, tower_weight))
    moved = []
    for half in halves:
        moved += [half, swapped(half, 1)]
    listings = listed_slot.shape[0]
    owner_ids = listed_owner[:, 0]
    served_by = serving_device(owner_ids, listed_slot)
    order = jnp.arange(listings, dtype=jnp.int32)
    same_device = served_by[:, None] == served_by[None, :]
    earlier = order[None, :] < order[:, None]
    rank_within = jnp.sum(jnp.logical_and(same_device, earlier), axis=1)
    device_match = served_by[:, None] == jnp.arange(owner_count, dtype=jnp.int32)[None, :]
    place = group * listings + order
    column = jnp.arange(1 + 2 * MOST, dtype=jnp.int32)[None, :]
    value = jnp.where(
        column == 0,
        1,
        jnp.where(column == 1 + rank_within[:, None], listed_slot[:, None], 0)
        + jnp.where(column == 1 + MOST + rank_within[:, None], place[:, None], 0),
    )
    codes = jnp.sum(
        jnp.where(device_match[:, :, None], value[:, None, :], 0), axis=0
    ).astype(BF)

    row_match = user_ids[:, None] == jnp.arange(UTAB, dtype=jnp.int32)[None, :]
    user_rows = jnp.dot(row_match.astype(BF), user_table, preferred_element_type=F32)
    user_rows = (user_rows * (1.0 / math.sqrt(H))).astype(BF).reshape(USERS * K, H)
    positives = positive_item.T
    marks = jnp.concatenate([positives // BLK, positives % BLK], axis=1).astype(BF)
    own = jnp.concatenate([user_rows, jnp.pad(marks, ((0, 0), (0, H - 2 * USERS)))], axis=0)
    pieces = [own] + [swapped(own, by) for by in range(1, GROUPS)]
    rows = [piece[: USERS * K] for piece in pieces]
    marks = [piece[USERS * K :] for piece in pieces]
    packed = jnp.concatenate(
        [jnp.concatenate(rows[0:2], axis=0), jnp.concatenate(rows[2:4], axis=0)], axis=1
    )
    meta = jnp.concatenate(
        [m[:, :USERS] for m in marks] + [m[:, USERS : 2 * USERS] for m in marks], axis=1
    )
    meta = jnp.pad(meta, ((0, 0), (0, 2 * H - 2 * CIRCLE_USERS)))
    common = jnp.concatenate([packed, meta], axis=0)
    sent = jnp.broadcast_to(common[None], (owner_count,) + common.shape)
    codes = jnp.pad(
        codes[:, None, :],
        ((0, 0), (ROWS // 2, 15), (2 * CIRCLE_USERS, 2 * H - 2 * CIRCLE_USERS - 1 - 2 * MOST)),
    )
    arrived = lax.all_to_all(sent + codes, "shard", split_axis=0, concat_axis=0, tiled=True)
    asked = arrived[:, ROWS // 2, 2 * CIRCLE_USERS : 2 * CIRCLE_USERS + 1 + 2 * MOST].astype(jnp.int32)

    vectors = (
        tower_vectors(tower_weight, item_features, None),
        tower_vectors(tower_weight, None, moved),
    )
    gates = (gate_in, gate_in_bias[None, :], gate_out.T, gate_out_bias[None, :])
    keep, send = pair_terms(
        asked, group[None], arrived, vectors, (item_features, *moved), gates
    )
    terms = (keep + swapped(send, 1).astype(F32)).astype(BF)
    terms = lax.all_to_all(terms, "shard", split_axis=0, concat_axis=0, tiled=True)
    sums = jnp.sum(terms.astype(F32), axis=0)
    rows = sums.shape[0] - K
    half = sums[:rows]
    from_1, from_2, from_3 = swapped(half, 1), swapped(sums, 2), swapped(half, 3)
    mine = half + from_2[:rows]
    other = from_1 + from_3
    even = group % 2 == 0
    tower_gradient = jnp.concatenate(
        [jnp.where(even, mine, other), jnp.where(even, other, mine)], axis=0
    )
    user_delta = sums[rows:, : USERS * H] + from_2[rows:, USERS * H :]
    user_delta = user_delta.reshape(K, USERS, H).transpose(1, 0, 2).reshape(USERS, E)
    user_gradient = split_product(row_match.astype(BF), user_delta)
    return (tower_gradient, user_gradient)


def solution(mesh):
    return jax.shard_map(
        shards,
        mesh=mesh,
        in_specs=(
            P("shard", None),
            P(),
            P(),
            P(),
            P(),
            P(),
            P(("blk", "shard"), None),
            P(("blk", "shard")),
            P(("blk", "shard"), None),
            P(("blk", "shard"), None),
            P(("blk", "shard")),
        ),
        out_specs=(P("shard", None), P(("blk", "shard"), None)),
        check_vma=False,
    )
```

```python
import math

import jax
import jax.numpy as jnp
from jax import lax
from jax.experimental import pallas as pl
from jax.experimental.pallas import tpu as pltpu
from jax.sharding import PartitionSpec as P

K = 8
H = 64
BLK = 128
CAP = 2
OWN = 32
STAY = 8
MOVE = 6
HALF = MOVE // 2
MOST = 5 * CAP
SIDE = 4
USERS = 4
TILE_USERS = 2
UTAB = 128
E = 512
GROUPS = 4
CIRCLE_USERS = GROUPS * USERS
ROWS = CIRCLE_USERS * K
PAIRS = K * K
F32 = jnp.float32
BF = jnp.bfloat16
VMEM_SPEC = pl.BlockSpec(memory_space=pltpu.VMEM)


def swapped(x, by):
    return lax.ppermute(x, "blk", [(i, i ^ by) for i in range(GROUPS)])


NEIGHBOURS = ((1, 1), (1, -1), (SIDE, 1), (SIDE, -1))


def neighbour(shard, stride, by):
    digit = shard // stride % SIDE
    return shard + ((digit + by) % SIDE - digit) * stride


def along(x, devices, stride, by):
    pairs = [(i, neighbour(i, stride, by)) for i in range(devices)]
    return lax.ppermute(x, "shard", pairs)


def serving_device(owner, slot):
    device = owner
    for i, (stride, by) in enumerate(NEIGHBOURS):
        here = jnp.logical_and(slot >= STAY + i * MOVE, slot < STAY + (i + 1) * MOVE)
        device = jnp.where(here, neighbour(owner, stride, by), device)
    return device


def tower_kernel(weight, *refs):
    out = refs[-1]
    blocks = out.shape[0] // (len(refs) - 1)
    for part, features in enumerate(refs[:-1]):
        product = jnp.dot(features[...], weight[...], preferred_element_type=F32).astype(BF)
        for c in range(blocks):
            turned = product[c * BLK : (c + 1) * BLK, :].T
            for b in range(K):
                out[part * blocks + c, :, b * BLK : (b + 1) * BLK] = turned[
                    b * H : (b + 1) * H, :
                ]


def tower_vectors(weight, stay, parts):
    width = weight.shape[0]
    if stay is not None:
        blocks = 8
        grid = (STAY // blocks,)
        operands = [stay]
        specs = [pl.BlockSpec((blocks * BLK, width), lambda i: (i, 0))]
    else:
        blocks = HALF * len(parts)
        grid = (1,)
        operands = parts
        specs = [pl.BlockSpec((HALF * BLK, width), lambda i: (0, 0))] * len(parts)
    total = blocks * grid[0]
    return pl.pallas_call(
        tower_kernel,
        grid=grid,
        in_specs=[pl.BlockSpec((width, E), lambda i: (0, 0))] + specs,
        out_specs=pl.BlockSpec((blocks, H, K * BLK), lambda i: (i, 0, 0)),
        out_shape=jax.ShapeDtypeStruct((total, H, K * BLK), BF),
        compiler_params=pltpu.CompilerParams(vmem_limit_bytes=58 << 20),
        cost_estimate=pl.CostEstimate(
            flops=2 * total * BLK * E * width, bytes_accessed=7 << 20, transcendentals=0
        ),
        name="tower_stay" if stay is not None else "tower_moved",
    )(weight, *operands)


def pair_kernel(codes, group, arrived_any, vt_stay, vt_moved, features_stay, moved_0, moved_1,
                moved_2, moved_3, moved_4, moved_5, moved_6, moved_7, gate_in, gate_in_bias, gate_out_t, gate_out_bias, keep, send, first_half, first, second_t, second_half,
                bias1, bias2, arrived, vt, features, grads, deltas, total,
                entry_slot, entry_shard, entry_start, sems, *buffers):
    step_rows = HALF * BLK
    moved = (moved_0, moved_1, moved_2, moved_3, moved_4, moved_5, moved_6, moved_7)
    pieces = [
        (arrived_any, arrived),
        (vt_stay, vt.at[pl.ds(0, STAY)]),
        (vt_moved, vt.at[pl.ds(STAY, OWN - STAY)]),
        (features_stay.at[pl.ds(0, STAY * BLK), :], features.at[pl.ds(0, STAY * BLK), :]),
    ] + [
        (part, features.at[pl.ds(STAY * BLK + i * step_rows, step_rows), :])
        for i, part in enumerate(moved)
    ]
    copies = [
        pltpu.make_async_copy(source, target, sems.at[i])
        for i, (source, target) in enumerate(pieces)
    ]
    for copy in copies[:3]:
        copy.start()
    owners = codes.shape[0]
    logits, hidden, slope, weights, back, pair_grad = [
        buffers[2 * i : 2 * i + 2] for i in range(6)
    ]
    tile = TILE_USERS * BLK
    tiles = CIRCLE_USERS // TILE_USERS

    def idle(position):
        entry_slot[position] = OWN
        entry_shard[position] = owners
        entry_start[position] = 0

    def enter_shard(shard, count):
        def enter(rank, position):
            slot = codes[shard, 1 + rank]
            upper = jnp.maximum(slot - STAY, 0) // HALF % 2
            turn = jnp.where(upper == 0, HALF, -HALF) * (group[0] & 1)
            entry_slot[position + 2] = slot + jnp.where(slot >= STAY, turn, 0)
            entry_shard[position + 2] = shard
            entry_start[position + 2] = codes[shard, 1 + MOST + rank] * BLK
            return position + 1

        return lax.fori_loop(0, jnp.minimum(codes[shard, 0], MOST), enter, count)

    count = lax.fori_loop(0, owners, enter_shard, 0)
    for position in (0, 1, count + 2, count + 3, count + 4):
        idle(position)
    grads[...] = jnp.zeros_like(grads)
    deltas[...] = jnp.zeros_like(deltas)
    lane = lax.broadcasted_iota(jnp.int32, (16, BLK), 1).astype(F32)
    row = lax.broadcasted_iota(jnp.int32, (PAIRS, PAIRS), 0)
    column = lax.broadcasted_iota(jnp.int32, (PAIRS, PAIRS), 1)
    order = jnp.where(column == (row & (K - 1)) * K + (row >> 3), 1.0, 0.0).astype(BF)
    across = (((1,), (1,)), ((), ()))
    turned_in = jnp.dot(order, gate_in[...], preferred_element_type=F32)
    turned_out = jnp.dot(order, gate_out_t[...], preferred_element_type=F32)
    first[...] = turned_in.astype(BF)
    first_half[...] = (turned_in.T * 0.5).astype(BF)
    second_t[...] = turned_out.astype(BF)
    second_half[...] = (turned_out.T * 0.5).astype(BF)
    bias1[...] = jnp.broadcast_to(gate_in_bias[...].astype(F32) * 0.5, bias1.shape).T
    bias2[...] = lax.dot_general(
        order,
        jnp.broadcast_to(gate_out_bias[...], (BLK, PAIRS)),
        across,
        preferred_element_type=F32,
    )
    for copy in copies[:3]:
        copy.wait()
    for copy in copies[3:]:
        copy.start()

    def users_of(shard):
        packed = arrived[jnp.minimum(shard, owners - 1), 0 : ROWS // 2, :]
        return jnp.concatenate([packed[:, :H], packed[:, H:]], axis=0)

    def items_of(slot):
        return vt[jnp.minimum(slot, OWN - 1)]

    def logits_of(ref, k):
        return jnp.concatenate(
            [
                jnp.concatenate(
                    [ref[u * K : (u + 1) * K, b * BLK : (b + 1) * BLK] for b in range(K)],
                    axis=0,
                )
                for u in range(TILE_USERS * k, TILE_USERS * (k + 1))
            ],
            axis=1,
        )

    def stages(n, even):
        odd = 1 - even
        start_slot, start_shard = entry_slot[n + 2], entry_shard[n + 2]
        middle_shard, middle_start = entry_shard[n + 1], entry_start[n + 1]
        end_slot, end_shard = entry_slot[n], entry_shard[n]
        meta = arrived[jnp.minimum(middle_shard, owners - 1), ROWS // 2 : ROWS // 2 + 16, :]
        meta = meta.astype(F32)
        offset = meta[:, 0:16] * BLK + meta[:, 16:32] - middle_start.astype(F32)

        def scores():
            logits[even][...] = jnp.dot(
                users_of(start_shard), items_of(start_slot), preferred_element_type=F32
            )

        def forward(k):
            columns = slice(k * tile, (k + 1) * tile)
            h = jnp.dot(
                first_half[...],
                logits_of(logits[even], k).astype(BF),
                preferred_element_type=F32,
            ) + jnp.concatenate([bias1[...]] * TILE_USERS, axis=1)
            t = jnp.tanh(h)
            q = 1.0 + t
            silu = h * q
            hidden[even][:, columns] = silu.astype(BF)
            slope[even][:, columns] = q + silu * (1.0 - t)

        def mix(k):
            columns = slice(k * tile, (k + 1) * tile)
            users = range(TILE_USERS * k, TILE_USERS * (k + 1))
            y = jnp.concatenate(
                [
                    jnp.max(
                        jnp.where(offset[:, u : u + 1] == lane, 1.0, 0.0), axis=0, keepdims=True
                    )
                    for u in users
                ],
                axis=1,
            )
            gate = jnp.dot(
                second_t[...], hidden[odd][:, columns], preferred_element_type=F32
            ) + jnp.concatenate([bias2[...]] * TILE_USERS, axis=1)
            e = jnp.exp(gate)
            lk = logits_of(logits[odd], k)
            inverse = 1.0 / jnp.sum(e, axis=0, keepdims=True)
            score = jnp.sum(e * lk, axis=0, keepdims=True) * inverse
            score_grad = 0.5 + 0.5 * jnp.tanh(0.5 * score) - y
            weighted = e * (score_grad * inverse)
            weights[odd][:, columns] = weighted
            return (weighted * (lk - score)).astype(BF)

        def gate_back(k, logit_grad):
            columns = slice(k * tile, (k + 1) * tile)
            hidden_grad = jnp.dot(second_half[...], logit_grad, preferred_element_type=F32)
            back[odd][:, columns] = (hidden_grad * slope[odd][:, columns]).astype(BF)

        def pair_back(k):
            columns = slice(k * tile, (k + 1) * tile)
            pg = jnp.dot(first[...], back[even][:, columns], preferred_element_type=F32)
            pg = pg + weights[even][:, columns]
            rows = slice(K * TILE_USERS * k, K * TILE_USERS * (k + 1))
            for b in range(K):
                pair_grad[even][rows, b * BLK : (b + 1) * BLK] = jnp.concatenate(
                    [
                        pg[b * K : (b + 1) * K, w * BLK : (w + 1) * BLK]
                        for w in range(TILE_USERS)
                    ],
                    axis=0,
                ).astype(BF)

        for k in range(tiles):
            pair_back(k)
        scores()
        logit_grads = [mix(k) for k in range(tiles)]
        pgv = pair_grad[even][...]
        deltas[end_shard] += lax.dot_general(
            pgv, items_of(end_slot), (((1,), (1,)), ((), ())), preferred_element_type=F32
        )
        grads[end_slot] += jnp.dot(users_of(end_shard).T, pgv, preferred_element_type=F32)
        for k in range(tiles):
            forward(k)
            gate_back(k, logit_grads[k])

    def step(i, carry):
        stages(2 * i, 0)
        stages(2 * i + 1, 1)
        return carry

    lax.fori_loop(0, (count + 3) // 2, step, 0)

    rows = keep.shape[1] - K
    scaling = 1.0 / math.sqrt(H)
    piece = USERS * K
    for c in range(2 * USERS):
        columns = slice(c * H, (c + 1) * H)
        first_row = 2 * piece * (c // USERS) + K * (c % USERS)
        keep[:, rows:, columns] = deltas[0:owners, first_row : first_row + K, :] * scaling
        first_row = first_row + piece
        send[:, rows:, columns] = (
            deltas[0:owners, first_row : first_row + K, :] * scaling
        ).astype(BF)
    for copy in copies[3:]:
        copy.wait()
    blocks = 8

    def add(i, carry):
        left = jnp.concatenate(
            [
                jnp.concatenate(
                    [
                        grads[i * blocks + c, :, b * BLK : (b + 1) * BLK].astype(BF)
                        for b in range(K)
                    ],
                    axis=0,
                )
                for c in range(blocks)
            ],
            axis=1,
        )
        start = pl.multiple_of(i * blocks * BLK, blocks * BLK)
        product = jnp.dot(
            left, features[pl.ds(start, blocks * BLK), :], preferred_element_type=F32
        )

        @pl.when(i == 0)
        def _():
            total[...] = product

        @pl.when(i > 0)
        def _():
            total[...] += product

        return carry

    lax.fori_loop(0, OWN // blocks, add, 0)
    parity = group[0] & 1
    for part in range(total.shape[1] // BLK):
        turned = total[:, part * BLK : (part + 1) * BLK].T
        for c in range(BLK // (2 * rows)):
            lower = turned[2 * rows * c : 2 * rows * c + rows, :]
            upper = turned[2 * rows * c + rows : 2 * rows * (c + 1), :]
            owner = part * (BLK // (2 * rows)) + c
            keep[owner, 0:rows, :] = jnp.where(parity == 0, lower, upper)
            send[owner, 0:rows, :] = jnp.where(parity == 0, upper, lower).astype(BF)


def pair_terms(codes, group, arrived, vectors, features, gates):
    owners = codes.shape[0]
    width = features[0].shape[1]
    any_spec = pl.BlockSpec(memory_space=pl.ANY)
    columns = CIRCLE_USERS * BLK
    hidden = gates[0].shape[1]
    shape = (owners, width // (2 * owners) + K, E)
    smem = pl.BlockSpec(memory_space=pltpu.SMEM)

    def twice(shape, dtype):
        return [pltpu.VMEM(shape, dtype)] * 2

    return pl.pallas_call(
        pair_kernel,
        out_shape=(jax.ShapeDtypeStruct(shape, F32), jax.ShapeDtypeStruct(shape, BF)),
        in_specs=[smem] * 2 + [any_spec] * 12 + [VMEM_SPEC] * 4,
        out_specs=(VMEM_SPEC, VMEM_SPEC),
        scratch_shapes=[
            pltpu.VMEM((hidden, PAIRS), BF),
            pltpu.VMEM((PAIRS, hidden), BF),
            pltpu.VMEM((PAIRS, hidden), BF),
            pltpu.VMEM((hidden, PAIRS), BF),
            pltpu.VMEM((hidden, BLK), F32),
            pltpu.VMEM((PAIRS, BLK), F32),
            pltpu.VMEM(arrived.shape, BF),
            pltpu.VMEM((OWN, H, K * BLK), BF),
            pltpu.VMEM((OWN * BLK, width), BF),
            pltpu.VMEM((OWN + 1, H, K * BLK), F32),
            pltpu.VMEM((owners + 1, ROWS, H), F32),
            pltpu.VMEM((E, width), F32),
            pltpu.SMEM((owners * MOST + 8,), jnp.int32),
            pltpu.SMEM((owners * MOST + 8,), jnp.int32),
            pltpu.SMEM((owners * MOST + 8,), jnp.int32),
            pltpu.SemaphoreType.DMA((12,)),
        ]
        + twice((ROWS, K * BLK), F32)
        + twice((hidden, columns), BF)
        + twice((hidden, columns), F32)
        + twice((PAIRS, columns), F32)
        + twice((hidden, columns), BF)
        + twice((ROWS, K * BLK), BF),
        compiler_params=pltpu.CompilerParams(vmem_limit_bytes=58 << 20),
        cost_estimate=pl.CostEstimate(
            flops=40 << 30, bytes_accessed=16 << 20, transcendentals=1 << 24
        ),
        name="pairs",
    )(codes, group, arrived, *vectors, *features, *gates)


def split_product(left_bf16, right_f32):
    upper = right_f32.astype(BF)
    lower = (right_f32 - upper.astype(F32)).astype(BF)
    dims = (((0,), (0,)), ((), ()))
    first = lax.dot_general(left_bf16, upper, dims, preferred_element_type=F32)
    second = lax.dot_general(left_bf16, lower, dims, preferred_element_type=F32)
    return first + second


def shards(
    item_features,
    tower_weight,
    gate_in,
    gate_in_bias,
    gate_out,
    gate_out_bias,
    user_table,
    user_ids,
    positive_item,
    listed_owner,
    listed_slot,
):
    owner_count = lax.axis_size("shard")
    group = lax.axis_index("blk")
    halves = []
    for i, (stride, by) in enumerate(NEIGHBOURS):
        first = (STAY + i * MOVE + group % 2 * HALF) * BLK
        half = lax.dynamic_slice_in_dim(item_features, first, HALF * BLK, axis=0)
        halves.append(along(half, owner_count, stride, by))
    halves, tower_weight = lax.optimization_barrier((halves, tower_weight))
    moved = []
    for half in halves:
        moved += [half, swapped(half, 1)]
    listings = listed_slot.shape[0]
    owner_ids = listed_owner[:, 0]
    served_by = serving_device(owner_ids, listed_slot)
    order = jnp.arange(listings, dtype=jnp.int32)
    same_device = served_by[:, None] == served_by[None, :]
    earlier = order[None, :] < order[:, None]
    rank_within = jnp.sum(jnp.logical_and(same_device, earlier), axis=1)
    device_match = served_by[:, None] == jnp.arange(owner_count, dtype=jnp.int32)[None, :]
    place = group * listings + order
    column = jnp.arange(1 + 2 * MOST, dtype=jnp.int32)[None, :]
    value = jnp.where(
        column == 0,
        1,
        jnp.where(column == 1 + rank_within[:, None], listed_slot[:, None], 0)
        + jnp.where(column == 1 + MOST + rank_within[:, None], place[:, None], 0),
    )
    codes = jnp.sum(
        jnp.where(device_match[:, :, None], value[:, None, :], 0), axis=0
    ).astype(BF)

    row_match = user_ids[:, None] == jnp.arange(UTAB, dtype=jnp.int32)[None, :]
    user_rows = jnp.dot(row_match.astype(BF), user_table, preferred_element_type=F32)
    user_rows = (user_rows * (1.0 / math.sqrt(H))).astype(BF).reshape(USERS * K, H)
    positives = positive_item.T
    marks = jnp.concatenate([positives // BLK, positives % BLK], axis=1).astype(BF)
    own = jnp.concatenate([user_rows, jnp.pad(marks, ((0, 0), (0, H - 2 * USERS)))], axis=0)
    pieces = [own] + [swapped(own, by) for by in range(1, GROUPS)]
    rows = [piece[: USERS * K] for piece in pieces]
    marks = [piece[USERS * K :] for piece in pieces]
    packed = jnp.concatenate(
        [jnp.concatenate(rows[0:2], axis=0), jnp.concatenate(rows[2:4], axis=0)], axis=1
    )
    meta = jnp.concatenate(
        [m[:, :USERS] for m in marks] + [m[:, USERS : 2 * USERS] for m in marks], axis=1
    )
    meta = jnp.pad(meta, ((0, 0), (0, 2 * H - 2 * CIRCLE_USERS)))
    common = jnp.concatenate([packed, meta], axis=0)
    sent = jnp.broadcast_to(common[None], (owner_count,) + common.shape)
    codes = jnp.pad(
        codes[:, None, :],
        ((0, 0), (ROWS // 2, 15), (2 * CIRCLE_USERS, 2 * H - 2 * CIRCLE_USERS - 1 - 2 * MOST)),
    )
    arrived = lax.all_to_all(sent + codes, "shard", split_axis=0, concat_axis=0, tiled=True)
    asked = arrived[:, ROWS // 2, 2 * CIRCLE_USERS : 2 * CIRCLE_USERS + 1 + 2 * MOST].astype(jnp.int32)

    vectors = (
        tower_vectors(tower_weight, item_features, None),
        tower_vectors(tower_weight, None, moved),
    )
    gates = (gate_in, gate_in_bias[None, :], gate_out.T, gate_out_bias[None, :])
    keep, send = pair_terms(
        asked, group[None], arrived, vectors, (item_features, *moved), gates
    )
    terms = (keep + swapped(send, 1).astype(F32)).astype(BF)
    terms = lax.all_to_all(terms, "shard", split_axis=0, concat_axis=0, tiled=True)
    sums = jnp.sum(terms.astype(F32), axis=0)
    rows = sums.shape[0] - K
    half = sums[:rows]
    from_1, from_2, from_3 = swapped(half, 1), swapped(sums, 2), swapped(half, 3)
    mine = half + from_2[:rows]
    other = from_1 + from_3
    even = group % 2 == 0
    tower_gradient = jnp.concatenate(
        [jnp.where(even, mine, other), jnp.where(even, other, mine)], axis=0
    )
    user_delta = sums[rows:, : USERS * H] + from_2[rows:, USERS * H :]
    user_delta = user_delta.reshape(K, USERS, H).transpose(1, 0, 2).reshape(USERS, E)
    user_gradient = split_product(row_match.astype(BF), user_delta)
    return (tower_gradient, user_gradient)


def solution(mesh):
    return jax.shard_map(
        shards,
        mesh=mesh,
        in_specs=(
            P("shard", None),
            P(),
            P(),
            P(),
            P(),
            P(),
            P(("blk", "shard"), None),
            P(("blk", "shard")),
            P(("blk", "shard"), None),
            P(("blk", "shard"), None),
            P(("blk", "shard")),
        ),
        out_specs=(P("shard", None), P(("blk", "shard"), None)),
        check_vma=False,
    )
```

```python
import math

import jax
import jax.numpy as jnp
from jax import lax
from jax.experimental import pallas as pl
from jax.experimental.pallas import tpu as pltpu
from jax.sharding import PartitionSpec as P

K = 8
H = 64
BLK = 128
CAP = 2
OWN = 32
STAY = 16
MOVE = 4
HALF = MOVE // 2
MOST = 5 * CAP
SIDE = 4
USERS = 4
TILE_USERS = 2
UTAB = 128
E = 512
GROUPS = 4
CIRCLE_USERS = GROUPS * USERS
ROWS = CIRCLE_USERS * K
PAIRS = K * K
F32 = jnp.float32
BF = jnp.bfloat16
VMEM_SPEC = pl.BlockSpec(memory_space=pltpu.VMEM)


def swapped(x, by):
    return lax.ppermute(x, "blk", [(i, i ^ by) for i in range(GROUPS)])


NEIGHBOURS = ((1, 1), (1, -1), (SIDE, 1), (SIDE, -1))


def neighbour(shard, stride, by):
    digit = shard // stride % SIDE
    return shard + ((digit + by) % SIDE - digit) * stride


def along(x, devices, stride, by):
    pairs = [(i, neighbour(i, stride, by)) for i in range(devices)]
    return lax.ppermute(x, "shard", pairs)


def serving_device(owner, slot):
    device = owner
    for i, (stride, by) in enumerate(NEIGHBOURS):
        here = jnp.logical_and(slot >= STAY + i * MOVE, slot < STAY + (i + 1) * MOVE)
        device = jnp.where(here, neighbour(owner, stride, by), device)
    return device


def project(features, weight, out, first):
    product = jnp.dot(features, weight, preferred_element_type=F32).astype(BF)
    for c in range(features.shape[0] // BLK):
        turned = product[c * BLK : (c + 1) * BLK, :].T
        for b in range(K):
            out[first + c, :, b * BLK : (b + 1) * BLK] = turned[b * H : (b + 1) * H, :]


def tower_kernel(weight, features, out):
    project(features[...], weight[...], out, 0)


def tower_vectors(weight, features):
    width = weight.shape[0]
    blocks = 8
    return pl.pallas_call(
        tower_kernel,
        grid=(STAY // blocks,),
        in_specs=[
            pl.BlockSpec((width, E), lambda i: (0, 0)),
            pl.BlockSpec((blocks * BLK, width), lambda i: (i, 0)),
        ],
        out_specs=pl.BlockSpec((blocks, H, K * BLK), lambda i: (i, 0, 0)),
        out_shape=jax.ShapeDtypeStruct((STAY, H, K * BLK), BF),
        compiler_params=pltpu.CompilerParams(vmem_limit_bytes=58 << 20),
        cost_estimate=pl.CostEstimate(
            flops=2 * STAY * BLK * E * width, bytes_accessed=7 << 20, transcendentals=0
        ),
        name="tower_stay",
    )(weight, features)


def pair_kernel(codes, group, arrived_any, vt_stay, weight, features_stay, moved_0, moved_1,
                moved_2, moved_3, moved_4, moved_5, moved_6, moved_7, gate_in, gate_in_bias, gate_out_t, gate_out_bias, keep, send, first_half, first, second_t, second_half,
                bias1, bias2, arrived, vt, features, grads, deltas, total,
                entry_slot, entry_shard, entry_start, sems, *buffers):
    step_rows = HALF * BLK
    moved = (moved_0, moved_1, moved_2, moved_3, moved_4, moved_5, moved_6, moved_7)
    pieces = [
        (part, features.at[pl.ds(STAY * BLK + i * step_rows, step_rows), :])
        for i, part in enumerate(moved)
    ] + [
        (arrived_any, arrived),
        (vt_stay, vt.at[pl.ds(0, STAY)]),
        (features_stay.at[pl.ds(0, STAY * BLK), :], features.at[pl.ds(0, STAY * BLK), :]),
    ]
    copies = [
        pltpu.make_async_copy(source, target, sems.at[i])
        for i, (source, target) in enumerate(pieces)
    ]
    for copy in copies:
        copy.start()
    owners = codes.shape[0]
    logits, hidden, slope, weights, back, pair_grad = [
        buffers[2 * i : 2 * i + 2] for i in range(6)
    ]
    tile = TILE_USERS * BLK
    tiles = CIRCLE_USERS // TILE_USERS

    def idle(position):
        entry_slot[position] = OWN
        entry_shard[position] = owners
        entry_start[position] = 0

    def enter_shard(shard, count):
        def enter(rank, position):
            slot = codes[shard, 1 + rank]
            upper = jnp.maximum(slot - STAY, 0) // HALF % 2
            turn = jnp.where(upper == 0, HALF, -HALF) * (group[0] & 1)
            entry_slot[position + 2] = slot + jnp.where(slot >= STAY, turn, 0)
            entry_shard[position + 2] = shard
            entry_start[position + 2] = codes[shard, 1 + MOST + rank] * BLK
            return position + 1

        return lax.fori_loop(0, jnp.minimum(codes[shard, 0], MOST), enter, count)

    count = lax.fori_loop(0, owners, enter_shard, 0)
    for position in (0, 1, count + 2, count + 3, count + 4):
        idle(position)
    grads[...] = jnp.zeros_like(grads)
    deltas[...] = jnp.zeros_like(deltas)
    lane = lax.broadcasted_iota(jnp.int32, (16, BLK), 1).astype(F32)
    row = lax.broadcasted_iota(jnp.int32, (PAIRS, PAIRS), 0)
    column = lax.broadcasted_iota(jnp.int32, (PAIRS, PAIRS), 1)
    order = jnp.where(column == (row & (K - 1)) * K + (row >> 3), 1.0, 0.0).astype(BF)
    across = (((1,), (1,)), ((), ()))
    turned_in = jnp.dot(order, gate_in[...], preferred_element_type=F32)
    turned_out = jnp.dot(order, gate_out_t[...], preferred_element_type=F32)
    first[...] = turned_in.astype(BF)
    first_half[...] = (turned_in.T * 0.5).astype(BF)
    second_t[...] = turned_out.astype(BF)
    second_half[...] = (turned_out.T * 0.5).astype(BF)
    bias1[...] = jnp.broadcast_to(gate_in_bias[...].astype(F32) * 0.5, bias1.shape).T
    bias2[...] = lax.dot_general(
        order,
        jnp.broadcast_to(gate_out_bias[...], (BLK, PAIRS)),
        across,
        preferred_element_type=F32,
    )
    for copy in copies[: len(moved)]:
        copy.wait()

    def form(i, carry):
        start = pl.multiple_of((STAY + i * MOVE) * BLK, MOVE * BLK)
        project(features[pl.ds(start, MOVE * BLK), :], weight[...], vt, STAY + i * MOVE)
        return carry

    lax.fori_loop(0, (OWN - STAY) // MOVE, form, 0)
    for copy in copies[len(moved) : -1]:
        copy.wait()

    def users_of(shard):
        packed = arrived[jnp.minimum(shard, owners - 1), 0 : ROWS // 2, :]
        return jnp.concatenate([packed[:, :H], packed[:, H:]], axis=0)

    def items_of(slot):
        return vt[jnp.minimum(slot, OWN - 1)]

    def logits_of(ref, k):
        return jnp.concatenate(
            [
                jnp.concatenate(
                    [ref[u * K : (u + 1) * K, b * BLK : (b + 1) * BLK] for b in range(K)],
                    axis=0,
                )
                for u in range(TILE_USERS * k, TILE_USERS * (k + 1))
            ],
            axis=1,
        )

    def stages(n, even):
        odd = 1 - even
        start_slot, start_shard = entry_slot[n + 2], entry_shard[n + 2]
        middle_shard, middle_start = entry_shard[n + 1], entry_start[n + 1]
        end_slot, end_shard = entry_slot[n], entry_shard[n]
        meta = arrived[jnp.minimum(middle_shard, owners - 1), ROWS // 2 : ROWS // 2 + 16, :]
        meta = meta.astype(F32)
        offset = meta[:, 0:16] * BLK + meta[:, 16:32] - middle_start.astype(F32)

        def scores():
            logits[even][...] = jnp.dot(
                users_of(start_shard), items_of(start_slot), preferred_element_type=F32
            )

        def forward(k):
            columns = slice(k * tile, (k + 1) * tile)
            h = jnp.dot(
                first_half[...],
                logits_of(logits[even], k).astype(BF),
                preferred_element_type=F32,
            ) + jnp.concatenate([bias1[...]] * TILE_USERS, axis=1)
            t = jnp.tanh(h)
            q = 1.0 + t
            silu = h * q
            hidden[even][:, columns] = silu.astype(BF)
            slope[even][:, columns] = q + silu * (1.0 - t)

        def mix(k):
            columns = slice(k * tile, (k + 1) * tile)
            users = range(TILE_USERS * k, TILE_USERS * (k + 1))
            y = jnp.concatenate(
                [
                    jnp.max(
                        jnp.where(offset[:, u : u + 1] == lane, 1.0, 0.0), axis=0, keepdims=True
                    )
                    for u in users
                ],
                axis=1,
            )
            gate = jnp.dot(
                second_t[...], hidden[odd][:, columns], preferred_element_type=F32
            ) + jnp.concatenate([bias2[...]] * TILE_USERS, axis=1)
            e = jnp.exp(gate)
            lk = logits_of(logits[odd], k)
            inverse = 1.0 / jnp.sum(e, axis=0, keepdims=True)
            score = jnp.sum(e * lk, axis=0, keepdims=True) * inverse
            score_grad = 0.5 + 0.5 * jnp.tanh(0.5 * score) - y
            weighted = e * (score_grad * inverse)
            weights[odd][:, columns] = weighted
            return (weighted * (lk - score)).astype(BF)

        def gate_back(k, logit_grad):
            columns = slice(k * tile, (k + 1) * tile)
            hidden_grad = jnp.dot(second_half[...], logit_grad, preferred_element_type=F32)
            back[odd][:, columns] = (hidden_grad * slope[odd][:, columns]).astype(BF)

        def pair_back(k):
            columns = slice(k * tile, (k + 1) * tile)
            pg = jnp.dot(first[...], back[even][:, columns], preferred_element_type=F32)
            pg = pg + weights[even][:, columns]
            rows = slice(K * TILE_USERS * k, K * TILE_USERS * (k + 1))
            for b in range(K):
                pair_grad[even][rows, b * BLK : (b + 1) * BLK] = jnp.concatenate(
                    [
                        pg[b * K : (b + 1) * K, w * BLK : (w + 1) * BLK]
                        for w in range(TILE_USERS)
                    ],
                    axis=0,
                ).astype(BF)

        for k in range(tiles):
            pair_back(k)
        scores()
        logit_grads = [mix(k) for k in range(tiles)]
        pgv = pair_grad[even][...]
        deltas[end_shard] += lax.dot_general(
            pgv, items_of(end_slot), (((1,), (1,)), ((), ())), preferred_element_type=F32
        )
        grads[end_slot] += jnp.dot(users_of(end_shard).T, pgv, preferred_element_type=F32)
        for k in range(tiles):
            forward(k)
            gate_back(k, logit_grads[k])

    def step(i, carry):
        stages(2 * i, 0)
        stages(2 * i + 1, 1)
        return carry

    lax.fori_loop(0, (count + 3) // 2, step, 0)

    rows = keep.shape[1] - K
    scaling = 1.0 / math.sqrt(H)
    piece = USERS * K
    for c in range(2 * USERS):
        columns = slice(c * H, (c + 1) * H)
        first_row = 2 * piece * (c // USERS) + K * (c % USERS)
        keep[:, rows:, columns] = deltas[0:owners, first_row : first_row + K, :] * scaling
        first_row = first_row + piece
        send[:, rows:, columns] = (
            deltas[0:owners, first_row : first_row + K, :] * scaling
        ).astype(BF)
    copies[-1].wait()
    blocks = 8

    def add(i, carry):
        left = jnp.concatenate(
            [
                jnp.concatenate(
                    [
                        grads[i * blocks + c, :, b * BLK : (b + 1) * BLK].astype(BF)
                        for b in range(K)
                    ],
                    axis=0,
                )
                for c in range(blocks)
            ],
            axis=1,
        )
        start = pl.multiple_of(i * blocks * BLK, blocks * BLK)
        product = jnp.dot(
            left, features[pl.ds(start, blocks * BLK), :], preferred_element_type=F32
        )

        @pl.when(i == 0)
        def _():
            total[...] = product

        @pl.when(i > 0)
        def _():
            total[...] += product

        return carry

    lax.fori_loop(0, OWN // blocks, add, 0)
    parity = group[0] & 1
    for part in range(total.shape[1] // BLK):
        turned = total[:, part * BLK : (part + 1) * BLK].T
        for c in range(BLK // (2 * rows)):
            lower = turned[2 * rows * c : 2 * rows * c + rows, :]
            upper = turned[2 * rows * c + rows : 2 * rows * (c + 1), :]
            owner = part * (BLK // (2 * rows)) + c
            keep[owner, 0:rows, :] = jnp.where(parity == 0, lower, upper)
            send[owner, 0:rows, :] = jnp.where(parity == 0, upper, lower).astype(BF)


def pair_terms(codes, group, arrived, vectors, features, gates):
    owners = codes.shape[0]
    width = features[0].shape[1]
    any_spec = pl.BlockSpec(memory_space=pl.ANY)
    columns = CIRCLE_USERS * BLK
    hidden = gates[0].shape[1]
    shape = (owners, width // (2 * owners) + K, E)
    smem = pl.BlockSpec(memory_space=pltpu.SMEM)

    def twice(shape, dtype):
        return [pltpu.VMEM(shape, dtype)] * 2

    return pl.pallas_call(
        pair_kernel,
        out_shape=(jax.ShapeDtypeStruct(shape, F32), jax.ShapeDtypeStruct(shape, BF)),
        in_specs=[smem] * 2 + [any_spec] * 2 + [VMEM_SPEC] + [any_spec] * 9 + [VMEM_SPEC] * 4,
        out_specs=(VMEM_SPEC, VMEM_SPEC),
        scratch_shapes=[
            pltpu.VMEM((hidden, PAIRS), BF),
            pltpu.VMEM((PAIRS, hidden), BF),
            pltpu.VMEM((PAIRS, hidden), BF),
            pltpu.VMEM((hidden, PAIRS), BF),
            pltpu.VMEM((hidden, BLK), F32),
            pltpu.VMEM((PAIRS, BLK), F32),
            pltpu.VMEM(arrived.shape, BF),
            pltpu.VMEM((OWN, H, K * BLK), BF),
            pltpu.VMEM((OWN * BLK, width), BF),
            pltpu.VMEM((OWN + 1, H, K * BLK), F32),
            pltpu.VMEM((owners + 1, ROWS, H), F32),
            pltpu.VMEM((E, width), F32),
            pltpu.SMEM((owners * MOST + 8,), jnp.int32),
            pltpu.SMEM((owners * MOST + 8,), jnp.int32),
            pltpu.SMEM((owners * MOST + 8,), jnp.int32),
            pltpu.SemaphoreType.DMA((11,)),
        ]
        + twice((ROWS, K * BLK), F32)
        + twice((hidden, columns), BF)
        + twice((hidden, columns), F32)
        + twice((PAIRS, columns), F32)
        + twice((hidden, columns), BF)
        + twice((ROWS, K * BLK), BF),
        compiler_params=pltpu.CompilerParams(vmem_limit_bytes=58 << 20),
        cost_estimate=pl.CostEstimate(
            flops=40 << 30, bytes_accessed=16 << 20, transcendentals=1 << 24
        ),
        name="pairs",
    )(codes, group, arrived, *vectors, *features, *gates)


def split_product(left_bf16, right_f32):
    upper = right_f32.astype(BF)
    lower = (right_f32 - upper.astype(F32)).astype(BF)
    dims = (((0,), (0,)), ((), ()))
    first = lax.dot_general(left_bf16, upper, dims, preferred_element_type=F32)
    second = lax.dot_general(left_bf16, lower, dims, preferred_element_type=F32)
    return first + second


def shards(
    item_features,
    tower_weight,
    gate_in,
    gate_in_bias,
    gate_out,
    gate_out_bias,
    user_table,
    user_ids,
    positive_item,
    listed_owner,
    listed_slot,
):
    owner_count = lax.axis_size("shard")
    group = lax.axis_index("blk")
    halves = []
    for i, (stride, by) in enumerate(NEIGHBOURS):
        first = (STAY + i * MOVE + group % 2 * HALF) * BLK
        half = lax.dynamic_slice_in_dim(item_features, first, HALF * BLK, axis=0)
        halves.append(along(half, owner_count, stride, by))
    halves, tower_weight = lax.optimization_barrier((halves, tower_weight))
    moved = []
    for half in halves:
        moved += [half, swapped(half, 1)]
    listings = listed_slot.shape[0]
    owner_ids = listed_owner[:, 0]
    served_by = serving_device(owner_ids, listed_slot)
    order = jnp.arange(listings, dtype=jnp.int32)
    same_device = served_by[:, None] == served_by[None, :]
    earlier = order[None, :] < order[:, None]
    rank_within = jnp.sum(jnp.logical_and(same_device, earlier), axis=1)
    device_match = served_by[:, None] == jnp.arange(owner_count, dtype=jnp.int32)[None, :]
    place = group * listings + order
    column = jnp.arange(1 + 2 * MOST, dtype=jnp.int32)[None, :]
    value = jnp.where(
        column == 0,
        1,
        jnp.where(column == 1 + rank_within[:, None], listed_slot[:, None], 0)
        + jnp.where(column == 1 + MOST + rank_within[:, None], place[:, None], 0),
    )
    codes = jnp.sum(
        jnp.where(device_match[:, :, None], value[:, None, :], 0), axis=0
    ).astype(BF)

    row_match = user_ids[:, None] == jnp.arange(UTAB, dtype=jnp.int32)[None, :]
    user_rows = jnp.dot(row_match.astype(BF), user_table, preferred_element_type=F32)
    user_rows = (user_rows * (1.0 / math.sqrt(H))).astype(BF).reshape(USERS * K, H)
    positives = positive_item.T
    marks = jnp.concatenate([positives // BLK, positives % BLK], axis=1).astype(BF)
    own = jnp.concatenate([user_rows, jnp.pad(marks, ((0, 0), (0, H - 2 * USERS)))], axis=0)
    pieces = [own] + [swapped(own, by) for by in range(1, GROUPS)]
    rows = [piece[: USERS * K] for piece in pieces]
    marks = [piece[USERS * K :] for piece in pieces]
    packed = jnp.concatenate(
        [jnp.concatenate(rows[0:2], axis=0), jnp.concatenate(rows[2:4], axis=0)], axis=1
    )
    meta = jnp.concatenate(
        [m[:, :USERS] for m in marks] + [m[:, USERS : 2 * USERS] for m in marks], axis=1
    )
    meta = jnp.pad(meta, ((0, 0), (0, 2 * H - 2 * CIRCLE_USERS)))
    common = jnp.concatenate([packed, meta], axis=0)
    sent = jnp.broadcast_to(common[None], (owner_count,) + common.shape)
    codes = jnp.pad(
        codes[:, None, :],
        ((0, 0), (ROWS // 2, 15), (2 * CIRCLE_USERS, 2 * H - 2 * CIRCLE_USERS - 1 - 2 * MOST)),
    )
    arrived = lax.all_to_all(sent + codes, "shard", split_axis=0, concat_axis=0, tiled=True)
    asked = arrived[:, ROWS // 2, 2 * CIRCLE_USERS : 2 * CIRCLE_USERS + 1 + 2 * MOST].astype(jnp.int32)

    vectors = (tower_vectors(tower_weight, item_features), tower_weight)
    gates = (gate_in, gate_in_bias[None, :], gate_out.T, gate_out_bias[None, :])
    keep, send = pair_terms(
        asked, group[None], arrived, vectors, (item_features, *moved), gates
    )
    terms = (keep + swapped(send, 1).astype(F32)).astype(BF)
    terms = lax.all_to_all(terms, "shard", split_axis=0, concat_axis=0, tiled=True)
    sums = jnp.sum(terms.astype(F32), axis=0)
    rows = sums.shape[0] - K
    half = sums[:rows]
    from_1, from_2, from_3 = swapped(half, 1), swapped(sums, 2), swapped(half, 3)
    mine = half + from_2[:rows]
    other = from_1 + from_3
    even = group % 2 == 0
    tower_gradient = jnp.concatenate(
        [jnp.where(even, mine, other), jnp.where(even, other, mine)], axis=0
    )
    user_delta = sums[rows:, : USERS * H] + from_2[rows:, USERS * H :]
    user_delta = user_delta.reshape(K, USERS, H).transpose(1, 0, 2).reshape(USERS, E)
    user_gradient = split_product(row_match.astype(BF), user_delta)
    return (tower_gradient, user_gradient)


def solution(mesh):
    return jax.shard_map(
        shards,
        mesh=mesh,
        in_specs=(
            P("shard", None),
            P(),
            P(),
            P(),
            P(),
            P(),
            P(("blk", "shard"), None),
            P(("blk", "shard")),
            P(("blk", "shard"), None),
            P(("blk", "shard"), None),
            P(("blk", "shard")),
        ),
        out_specs=(P("shard", None), P(("blk", "shard"), None)),
        check_vma=False,
    )
```

```python
import math

import jax
import jax.numpy as jnp
from jax import lax
from jax.experimental import pallas as pl
from jax.experimental.pallas import tpu as pltpu
from jax.sharding import PartitionSpec as P

K = 8
H = 64
BLK = 128
CAP = 2
OWN = 32
STAY = 14
MOVE = 4
HALF = MOVE // 2
LAST = 2
MOST = 6 * CAP
SIDE = 4
USERS = 4
TILE_USERS = 2
UTAB = 128
E = 512
GROUPS = 4
CIRCLE_USERS = GROUPS * USERS
ROWS = CIRCLE_USERS * K
PAIRS = K * K
F32 = jnp.float32
BF = jnp.bfloat16
VMEM_SPEC = pl.BlockSpec(memory_space=pltpu.VMEM)


def swapped(x, by):
    return lax.ppermute(x, "blk", [(i, i ^ by) for i in range(GROUPS)])


PARTS = (
    (STAY, MOVE, 1, SIDE, 1),
    (STAY + MOVE, MOVE, 1, SIDE, -1),
    (STAY + 2 * MOVE, MOVE, SIDE, SIDE, 1),
    (STAY + 3 * MOVE, MOVE, SIDE, SIDE, -1),
    (OWN - LAST, LAST, SIDE * SIDE, 2, 1),
)


def neighbour(shard, stride, base, by):
    digit = shard // stride % base
    return shard + ((digit + by) % base - digit) * stride


def along(x, devices, stride, base, by):
    pairs = [(i, neighbour(i, stride, base, by)) for i in range(devices)]
    return lax.ppermute(x, "shard", pairs)


def serving_device(owner, slot):
    device = owner
    for first, blocks, stride, base, by in PARTS:
        here = jnp.logical_and(slot >= first, slot < first + blocks)
        device = jnp.where(here, neighbour(owner, stride, base, by), device)
    return device


def project(features, weight, out, first):
    product = jnp.dot(features, weight, preferred_element_type=F32).astype(BF)
    for c in range(features.shape[0] // BLK):
        turned = product[c * BLK : (c + 1) * BLK, :].T
        for b in range(K):
            out[first + c, :, b * BLK : (b + 1) * BLK] = turned[b * H : (b + 1) * H, :]


def tower_kernel(weight, features, out):
    project(features[...], weight[...], out, 0)


def tower_vectors(weight, features):
    width = weight.shape[0]
    blocks = STAY // 2
    return pl.pallas_call(
        tower_kernel,
        grid=(STAY // blocks,),
        in_specs=[
            pl.BlockSpec((width, E), lambda i: (0, 0)),
            pl.BlockSpec((blocks * BLK, width), lambda i: (i, 0)),
        ],
        out_specs=pl.BlockSpec((blocks, H, K * BLK), lambda i: (i, 0, 0)),
        out_shape=jax.ShapeDtypeStruct((STAY, H, K * BLK), BF),
        compiler_params=pltpu.CompilerParams(vmem_limit_bytes=58 << 20),
        cost_estimate=pl.CostEstimate(
            flops=2 * STAY * BLK * E * width, bytes_accessed=7 << 20, transcendentals=0
        ),
        name="tower_stay",
    )(weight, features)


def pair_kernel(codes, group, arrived_any, vt_stay, weight, features_stay, moved_0, moved_1,
                moved_2, moved_3, moved_4, moved_5, moved_6, moved_7, moved_8,
                moved_9, gate_in, gate_in_bias, gate_out_t, gate_out_bias, keep, send, first_half, first, second_t, second_half,
                bias1, bias2, arrived, vt, features, grads, deltas, total,
                entry_slot, entry_shard, entry_start, sems, *buffers):
    moved = (moved_0, moved_1, moved_2, moved_3, moved_4, moved_5, moved_6, moved_7, moved_8,
             moved_9)
    places = [
        ((start + half * (blocks // 2)) * BLK, blocks // 2 * BLK)
        for start, blocks, _, _, _ in PARTS
        for half in range(2)
    ]
    pieces = [
        (part, features.at[pl.ds(start, size), :])
        for part, (start, size) in zip(moved, places)
    ] + [
        (arrived_any, arrived),
        (vt_stay, vt.at[pl.ds(0, STAY)]),
        (features_stay.at[pl.ds(0, STAY * BLK), :], features.at[pl.ds(0, STAY * BLK), :]),
    ]
    copies = [
        pltpu.make_async_copy(source, target, sems.at[i])
        for i, (source, target) in enumerate(pieces)
    ]
    for copy in copies[:-1]:
        copy.start()
    owners = codes.shape[0]
    logits, hidden, slope, weights, back, pair_grad = [
        buffers[2 * i : 2 * i + 2] for i in range(6)
    ]
    tile = TILE_USERS * BLK
    tiles = CIRCLE_USERS // TILE_USERS

    def idle(position):
        entry_slot[position] = OWN
        entry_shard[position] = owners
        entry_start[position] = 0

    def enter_shard(shard, count):
        def enter(rank, position):
            slot = codes[shard, 1 + rank]
            last = slot >= OWN - LAST
            upper = jnp.where(
                last,
                jnp.maximum(slot - (OWN - LAST), 0) // (LAST // 2),
                jnp.maximum(slot - STAY, 0) // HALF % 2,
            )
            half = jnp.where(last, LAST // 2, HALF)
            turn = jnp.where(upper == 0, half, -half) * (group[0] & 1)
            entry_slot[position + 2] = slot + jnp.where(slot >= STAY, turn, 0)
            entry_shard[position + 2] = shard
            entry_start[position + 2] = codes[shard, 1 + MOST + rank] * BLK
            return position + 1

        return lax.fori_loop(0, jnp.minimum(codes[shard, 0], MOST), enter, count)

    count = lax.fori_loop(0, owners, enter_shard, 0)
    for position in (0, 1, count + 2, count + 3, count + 4):
        idle(position)
    grads[...] = jnp.zeros_like(grads)
    deltas[...] = jnp.zeros_like(deltas)
    lane = lax.broadcasted_iota(jnp.int32, (16, BLK), 1).astype(F32)
    row = lax.broadcasted_iota(jnp.int32, (PAIRS, PAIRS), 0)
    column = lax.broadcasted_iota(jnp.int32, (PAIRS, PAIRS), 1)
    order = jnp.where(column == (row & (K - 1)) * K + (row >> 3), 1.0, 0.0).astype(BF)
    across = (((1,), (1,)), ((), ()))
    turned_in = jnp.dot(order, gate_in[...], preferred_element_type=F32)
    turned_out = jnp.dot(order, gate_out_t[...], preferred_element_type=F32)
    first[...] = turned_in.astype(BF)
    first_half[...] = (turned_in.T * 0.5).astype(BF)
    second_t[...] = turned_out.astype(BF)
    second_half[...] = (turned_out.T * 0.5).astype(BF)
    bias1[...] = jnp.broadcast_to(gate_in_bias[...].astype(F32) * 0.5, bias1.shape).T
    bias2[...] = lax.dot_general(
        order,
        jnp.broadcast_to(gate_out_bias[...], (BLK, PAIRS)),
        across,
        preferred_element_type=F32,
    )
    for copy in copies[: len(moved)]:
        copy.wait()
    copies[-1].start()

    def form(i, carry):
        start = pl.multiple_of((STAY + i * MOVE) * BLK, 2 * BLK)
        project(features[pl.ds(start, MOVE * BLK), :], weight[...], vt, STAY + i * MOVE)
        return carry

    lax.fori_loop(0, (OWN - LAST - STAY) // MOVE, form, 0)
    project(features[(OWN - LAST) * BLK :, :], weight[...], vt, OWN - LAST)
    for copy in copies[len(moved) : -1]:
        copy.wait()

    def users_of(shard):
        packed = arrived[jnp.minimum(shard, owners - 1), 0 : ROWS // 2, :]
        return jnp.concatenate([packed[:, :H], packed[:, H:]], axis=0)

    def items_of(slot):
        return vt[jnp.minimum(slot, OWN - 1)]

    def logits_of(ref, k):
        return jnp.concatenate(
            [
                jnp.concatenate(
                    [ref[u * K : (u + 1) * K, b * BLK : (b + 1) * BLK] for b in range(K)],
                    axis=0,
                )
                for u in range(TILE_USERS * k, TILE_USERS * (k + 1))
            ],
            axis=1,
        )

    def stages(n, even):
        odd = 1 - even
        start_slot, start_shard = entry_slot[n + 2], entry_shard[n + 2]
        middle_shard, middle_start = entry_shard[n + 1], entry_start[n + 1]
        end_slot, end_shard = entry_slot[n], entry_shard[n]
        meta = arrived[jnp.minimum(middle_shard, owners - 1), ROWS // 2 : ROWS // 2 + 16, :]
        meta = meta.astype(F32)
        offset = meta[:, 0:16] * BLK + meta[:, 16:32] - middle_start.astype(F32)

        def scores():
            logits[even][...] = jnp.dot(
                users_of(start_shard), items_of(start_slot), preferred_element_type=F32
            )

        def forward(k):
            columns = slice(k * tile, (k + 1) * tile)
            h = jnp.dot(
                first_half[...],
                logits_of(logits[even], k).astype(BF),
                preferred_element_type=F32,
            ) + jnp.concatenate([bias1[...]] * TILE_USERS, axis=1)
            t = jnp.tanh(h)
            q = 1.0 + t
            silu = h * q
            hidden[even][:, columns] = silu.astype(BF)
            slope[even][:, columns] = q + silu * (1.0 - t)

        def mix(k):
            columns = slice(k * tile, (k + 1) * tile)
            users = range(TILE_USERS * k, TILE_USERS * (k + 1))
            y = jnp.concatenate(
                [
                    jnp.max(
                        jnp.where(offset[:, u : u + 1] == lane, 1.0, 0.0), axis=0, keepdims=True
                    )
                    for u in users
                ],
                axis=1,
            )
            gate = jnp.dot(
                second_t[...], hidden[odd][:, columns], preferred_element_type=F32
            ) + jnp.concatenate([bias2[...]] * TILE_USERS, axis=1)
            e = jnp.exp(gate)
            lk = logits_of(logits[odd], k)
            inverse = 1.0 / jnp.sum(e, axis=0, keepdims=True)
            score = jnp.sum(e * lk, axis=0, keepdims=True) * inverse
            score_grad = 0.5 + 0.5 * jnp.tanh(0.5 * score) - y
            weighted = e * (score_grad * inverse)
            weights[odd][:, columns] = weighted
            return (weighted * (lk - score)).astype(BF)

        def gate_back(k, logit_grad):
            columns = slice(k * tile, (k + 1) * tile)
            hidden_grad = jnp.dot(second_half[...], logit_grad, preferred_element_type=F32)
            back[odd][:, columns] = (hidden_grad * slope[odd][:, columns]).astype(BF)

        def pair_back(k):
            columns = slice(k * tile, (k + 1) * tile)
            pg = jnp.dot(first[...], back[even][:, columns], preferred_element_type=F32)
            pg = pg + weights[even][:, columns]
            rows = slice(K * TILE_USERS * k, K * TILE_USERS * (k + 1))
            for b in range(K):
                pair_grad[even][rows, b * BLK : (b + 1) * BLK] = jnp.concatenate(
                    [
                        pg[b * K : (b + 1) * K, w * BLK : (w + 1) * BLK]
                        for w in range(TILE_USERS)
                    ],
                    axis=0,
                ).astype(BF)

        for k in range(tiles):
            pair_back(k)
        scores()
        logit_grads = [mix(k) for k in range(tiles)]
        pgv = pair_grad[even][...]
        deltas[end_shard] += lax.dot_general(
            pgv, items_of(end_slot), (((1,), (1,)), ((), ())), preferred_element_type=F32
        )
        grads[end_slot] += jnp.dot(users_of(end_shard).T, pgv, preferred_element_type=F32)
        for k in range(tiles):
            forward(k)
            gate_back(k, logit_grads[k])

    def step(i, carry):
        stages(2 * i, 0)
        stages(2 * i + 1, 1)
        return carry

    lax.fori_loop(0, (count + 3) // 2, step, 0)

    rows = keep.shape[1] - K
    scaling = 1.0 / math.sqrt(H)
    piece = USERS * K
    for c in range(2 * USERS):
        columns = slice(c * H, (c + 1) * H)
        first_row = 2 * piece * (c // USERS) + K * (c % USERS)
        keep[:, rows:, columns] = (
            deltas[0:owners, first_row : first_row + K, :] * scaling
        ).astype(BF)
        first_row = first_row + piece
        send[:, rows:, columns] = (
            deltas[0:owners, first_row : first_row + K, :] * scaling
        ).astype(BF)
    copies[-1].wait()
    blocks = 8

    def add(i, carry):
        left = jnp.concatenate(
            [
                jnp.concatenate(
                    [
                        grads[i * blocks + c, :, b * BLK : (b + 1) * BLK].astype(BF)
                        for b in range(K)
                    ],
                    axis=0,
                )
                for c in range(blocks)
            ],
            axis=1,
        )
        start = pl.multiple_of(i * blocks * BLK, blocks * BLK)
        product = jnp.dot(
            left, features[pl.ds(start, blocks * BLK), :], preferred_element_type=F32
        )

        @pl.when(i == 0)
        def _():
            total[...] = product

        @pl.when(i > 0)
        def _():
            total[...] += product

        return carry

    lax.fori_loop(0, OWN // blocks, add, 0)
    parity = group[0] & 1
    for part in range(total.shape[1] // BLK):
        turned = total[:, part * BLK : (part + 1) * BLK].T
        for c in range(BLK // (2 * rows)):
            lower = turned[2 * rows * c : 2 * rows * c + rows, :]
            upper = turned[2 * rows * c + rows : 2 * rows * (c + 1), :]
            owner = part * (BLK // (2 * rows)) + c
            keep[owner, 0:rows, :] = jnp.where(parity == 0, lower, upper).astype(BF)
            send[owner, 0:rows, :] = jnp.where(parity == 0, upper, lower).astype(BF)


def pair_terms(codes, group, arrived, vectors, features, gates):
    owners = codes.shape[0]
    width = features[0].shape[1]
    any_spec = pl.BlockSpec(memory_space=pl.ANY)
    columns = CIRCLE_USERS * BLK
    hidden = gates[0].shape[1]
    shape = (owners, width // (2 * owners) + K, E)
    smem = pl.BlockSpec(memory_space=pltpu.SMEM)

    def twice(shape, dtype):
        return [pltpu.VMEM(shape, dtype)] * 2

    return pl.pallas_call(
        pair_kernel,
        out_shape=(jax.ShapeDtypeStruct(shape, BF),) * 2,
        in_specs=[smem] * 2 + [any_spec] * 2 + [VMEM_SPEC] + [any_spec] * 11 + [VMEM_SPEC] * 4,
        out_specs=(VMEM_SPEC, VMEM_SPEC),
        scratch_shapes=[
            pltpu.VMEM((hidden, PAIRS), BF),
            pltpu.VMEM((PAIRS, hidden), BF),
            pltpu.VMEM((PAIRS, hidden), BF),
            pltpu.VMEM((hidden, PAIRS), BF),
            pltpu.VMEM((hidden, BLK), F32),
            pltpu.VMEM((PAIRS, BLK), F32),
            pltpu.VMEM(arrived.shape, BF),
            pltpu.VMEM((OWN, H, K * BLK), BF),
            pltpu.VMEM((OWN * BLK, width), BF),
            pltpu.VMEM((OWN + 1, H, K * BLK), F32),
            pltpu.VMEM((owners + 1, ROWS, H), F32),
            pltpu.VMEM((E, width), F32),
            pltpu.SMEM((owners * MOST + 8,), jnp.int32),
            pltpu.SMEM((owners * MOST + 8,), jnp.int32),
            pltpu.SMEM((owners * MOST + 8,), jnp.int32),
            pltpu.SemaphoreType.DMA((13,)),
        ]
        + twice((ROWS, K * BLK), F32)
        + twice((hidden, columns), BF)
        + twice((hidden, columns), F32)
        + twice((PAIRS, columns), F32)
        + twice((hidden, columns), BF)
        + twice((ROWS, K * BLK), BF),
        compiler_params=pltpu.CompilerParams(vmem_limit_bytes=58 << 20),
        cost_estimate=pl.CostEstimate(
            flops=40 << 30, bytes_accessed=16 << 20, transcendentals=1 << 24
        ),
        name="pairs",
    )(codes, group, arrived, *vectors, *features, *gates)


def split_product(left_bf16, right_f32):
    upper = right_f32.astype(BF)
    lower = (right_f32 - upper.astype(F32)).astype(BF)
    dims = (((0,), (0,)), ((), ()))
    first = lax.dot_general(left_bf16, upper, dims, preferred_element_type=F32)
    second = lax.dot_general(left_bf16, lower, dims, preferred_element_type=F32)
    return first + second


def shards(
    item_features,
    tower_weight,
    gate_in,
    gate_in_bias,
    gate_out,
    gate_out_bias,
    user_table,
    user_ids,
    positive_item,
    listed_owner,
    listed_slot,
):
    owner_count = lax.axis_size("shard")
    group = lax.axis_index("blk")
    halves = []
    for first, blocks, stride, base, by in PARTS:
        start = (first + group % 2 * (blocks // 2)) * BLK
        half = lax.dynamic_slice_in_dim(item_features, start, blocks // 2 * BLK, axis=0)
        halves.append(along(half, owner_count, stride, base, by))
    halves, tower_weight = lax.optimization_barrier((halves, tower_weight))
    moved = []
    for half in halves:
        moved += [half, swapped(half, 1)]
    listings = listed_slot.shape[0]
    owner_ids = listed_owner[:, 0]
    served_by = serving_device(owner_ids, listed_slot)
    order = jnp.arange(listings, dtype=jnp.int32)
    same_device = served_by[:, None] == served_by[None, :]
    earlier = order[None, :] < order[:, None]
    rank_within = jnp.sum(jnp.logical_and(same_device, earlier), axis=1)
    device_match = served_by[:, None] == jnp.arange(owner_count, dtype=jnp.int32)[None, :]
    place = group * listings + order
    column = jnp.arange(1 + 2 * MOST, dtype=jnp.int32)[None, :]
    value = jnp.where(
        column == 0,
        1,
        jnp.where(column == 1 + rank_within[:, None], listed_slot[:, None], 0)
        + jnp.where(column == 1 + MOST + rank_within[:, None], place[:, None], 0),
    )
    codes = jnp.sum(
        jnp.where(device_match[:, :, None], value[:, None, :], 0), axis=0
    ).astype(BF)

    row_match = user_ids[:, None] == jnp.arange(UTAB, dtype=jnp.int32)[None, :]
    user_rows = jnp.dot(row_match.astype(BF), user_table, preferred_element_type=F32)
    user_rows = (user_rows * (1.0 / math.sqrt(H))).astype(BF).reshape(USERS * K, H)
    positives = positive_item.T
    marks = jnp.concatenate([positives // BLK, positives % BLK], axis=1).astype(BF)
    own = jnp.concatenate([user_rows, jnp.pad(marks, ((0, 0), (0, H - 2 * USERS)))], axis=0)
    pieces = [own] + [swapped(own, by) for by in range(1, GROUPS)]
    rows = [piece[: USERS * K] for piece in pieces]
    marks = [piece[USERS * K :] for piece in pieces]
    packed = jnp.concatenate(
        [jnp.concatenate(rows[0:2], axis=0), jnp.concatenate(rows[2:4], axis=0)], axis=1
    )
    meta = jnp.concatenate(
        [m[:, :USERS] for m in marks] + [m[:, USERS : 2 * USERS] for m in marks], axis=1
    )
    meta = jnp.pad(meta, ((0, 0), (0, 2 * H - 2 * CIRCLE_USERS)))
    common = jnp.concatenate([packed, meta], axis=0)
    sent = jnp.broadcast_to(common[None], (owner_count,) + common.shape)
    codes = jnp.pad(
        codes[:, None, :],
        ((0, 0), (ROWS // 2, 15), (2 * CIRCLE_USERS, 2 * H - 2 * CIRCLE_USERS - 1 - 2 * MOST)),
    )
    arrived = lax.all_to_all(sent + codes, "shard", split_axis=0, concat_axis=0, tiled=True)
    asked = arrived[:, ROWS // 2, 2 * CIRCLE_USERS : 2 * CIRCLE_USERS + 1 + 2 * MOST].astype(jnp.int32)

    vectors = (tower_vectors(tower_weight, item_features), tower_weight)
    gates = (gate_in, gate_in_bias[None, :], gate_out.T, gate_out_bias[None, :])
    keep, send = pair_terms(
        asked, group[None], arrived, vectors, (item_features, *moved), gates
    )
    terms = (keep.astype(F32) + swapped(send, 1).astype(F32)).astype(BF)
    terms = lax.all_to_all(terms, "shard", split_axis=0, concat_axis=0, tiled=True)
    sums = jnp.sum(terms.astype(F32), axis=0)
    rows = sums.shape[0] - K
    half = sums[:rows]
    from_1, from_2, from_3 = swapped(half, 1), swapped(sums, 2), swapped(half, 3)
    mine = half + from_2[:rows]
    other = from_1 + from_3
    even = group % 2 == 0
    tower_gradient = jnp.concatenate(
        [jnp.where(even, mine, other), jnp.where(even, other, mine)], axis=0
    )
    user_delta = sums[rows:, : USERS * H] + from_2[rows:, USERS * H :]
    user_delta = user_delta.reshape(K, USERS, H).transpose(1, 0, 2).reshape(USERS, E)
    user_gradient = split_product(row_match.astype(BF), user_delta)
    return (tower_gradient, user_gradient)


def solution(mesh):
    return jax.shard_map(
        shards,
        mesh=mesh,
        in_specs=(
            P("shard", None),
            P(),
            P(),
            P(),
            P(),
            P(),
            P(("blk", "shard"), None),
            P(("blk", "shard")),
            P(("blk", "shard"), None),
            P(("blk", "shard"), None),
            P(("blk", "shard")),
        ),
        out_specs=(P("shard", None), P(("blk", "shard"), None)),
        check_vma=False,
    )
```

```python
import math

import jax
import jax.numpy as jnp
from jax import lax
from jax.experimental import pallas as pl
from jax.experimental.pallas import tpu as pltpu
from jax.sharding import PartitionSpec as P

K = 8
H = 64
BLK = 128
CAP = 2
OWN = 32
STAY = 16
MOVE = 4
HALF = MOVE // 2
MOST = 5 * CAP
SIDE = 4
USERS = 4
TILE_USERS = 2
UTAB = 128
E = 512
GROUPS = 4
CIRCLE_USERS = GROUPS * USERS
ROWS = CIRCLE_USERS * K
PAIRS = K * K
F32 = jnp.float32
BF = jnp.bfloat16
VMEM_SPEC = pl.BlockSpec(memory_space=pltpu.VMEM)


def swapped(x, by):
    return lax.ppermute(x, "blk", [(i, i ^ by) for i in range(GROUPS)])


NEIGHBOURS = ((1, 1), (1, -1), (SIDE, 1), (SIDE, -1))


def neighbour(shard, stride, by):
    digit = shard // stride % SIDE
    return shard + ((digit + by) % SIDE - digit) * stride


def along(x, devices, stride, by):
    pairs = [(i, neighbour(i, stride, by)) for i in range(devices)]
    return lax.ppermute(x, "shard", pairs)


def serving_device(owner, slot):
    device = owner
    for i, (stride, by) in enumerate(NEIGHBOURS):
        here = jnp.logical_and(slot >= STAY + i * MOVE, slot < STAY + (i + 1) * MOVE)
        device = jnp.where(here, neighbour(owner, stride, by), device)
    return device


def project(features, weight, out, first):
    product = jnp.dot(features, weight, preferred_element_type=F32).astype(BF)
    for c in range(features.shape[0] // BLK):
        turned = product[c * BLK : (c + 1) * BLK, :].T
        for b in range(K):
            out[first + c, :, b * BLK : (b + 1) * BLK] = turned[b * H : (b + 1) * H, :]


def tower_kernel(weight, features, out):
    project(features[...], weight[...], out, 0)


def tower_vectors(weight, features):
    width = weight.shape[0]
    blocks = 8
    return pl.pallas_call(
        tower_kernel,
        grid=(STAY // blocks,),
        in_specs=[
            pl.BlockSpec((width, E), lambda i: (0, 0)),
            pl.BlockSpec((blocks * BLK, width), lambda i: (i, 0)),
        ],
        out_specs=pl.BlockSpec((blocks, H, K * BLK), lambda i: (i, 0, 0)),
        out_shape=jax.ShapeDtypeStruct((STAY, H, K * BLK), BF),
        compiler_params=pltpu.CompilerParams(vmem_limit_bytes=58 << 20),
        cost_estimate=pl.CostEstimate(
            flops=2 * STAY * BLK * E * width, bytes_accessed=7 << 20, transcendentals=0
        ),
        name="tower_stay",
    )(weight, features)


def pair_kernel(codes, group, arrived_any, vt_stay, weight, features_stay, moved_0, moved_1,
                moved_2, moved_3, moved_4, moved_5, moved_6, moved_7, gate_in, gate_in_bias, gate_out_t, gate_out_bias, keep, send, first_half, first, second_t, second_half,
                bias1, bias2, arrived, vt, features, grads, deltas, total,
                entry_slot, entry_shard, entry_start, sems, *buffers):
    step_rows = HALF * BLK
    moved = (moved_0, moved_1, moved_2, moved_3, moved_4, moved_5, moved_6, moved_7)
    pieces = [
        (part, features.at[pl.ds(STAY * BLK + i * step_rows, step_rows), :])
        for i, part in enumerate(moved)
    ] + [
        (arrived_any, arrived),
        (vt_stay, vt.at[pl.ds(0, STAY)]),
        (features_stay.at[pl.ds(0, STAY * BLK), :], features.at[pl.ds(0, STAY * BLK), :]),
    ]
    copies = [
        pltpu.make_async_copy(source, target, sems.at[i])
        for i, (source, target) in enumerate(pieces)
    ]
    for copy in copies[:-1]:
        copy.start()
    owners = codes.shape[0]
    logits, hidden, slope, weights, back, pair_grad = [
        buffers[2 * i : 2 * i + 2] for i in range(6)
    ]
    tile = TILE_USERS * BLK
    tiles = CIRCLE_USERS // TILE_USERS

    def idle(position):
        entry_slot[position] = OWN
        entry_shard[position] = owners
        entry_start[position] = 0

    def enter_shard(shard, count):
        def enter(rank, position):
            slot = codes[shard, 1 + rank]
            upper = jnp.maximum(slot - STAY, 0) // HALF % 2
            turn = jnp.where(upper == 0, HALF, -HALF) * (group[0] & 1)
            entry_slot[position + 2] = slot + jnp.where(slot >= STAY, turn, 0)
            entry_shard[position + 2] = shard
            entry_start[position + 2] = codes[shard, 1 + MOST + rank] * BLK
            return position + 1

        return lax.fori_loop(0, jnp.minimum(codes[shard, 0], MOST), enter, count)

    count = lax.fori_loop(0, owners, enter_shard, 0)
    for position in (0, 1, count + 2, count + 3, count + 4):
        idle(position)
    grads[...] = jnp.zeros_like(grads)
    deltas[...] = jnp.zeros_like(deltas)
    lane = lax.broadcasted_iota(jnp.int32, (16, BLK), 1).astype(F32)
    row = lax.broadcasted_iota(jnp.int32, (PAIRS, PAIRS), 0)
    column = lax.broadcasted_iota(jnp.int32, (PAIRS, PAIRS), 1)
    order = jnp.where(column == (row & (K - 1)) * K + (row >> 3), 1.0, 0.0).astype(BF)
    across = (((1,), (1,)), ((), ()))
    turned_in = jnp.dot(order, gate_in[...], preferred_element_type=F32)
    turned_out = jnp.dot(order, gate_out_t[...], preferred_element_type=F32)
    first[...] = turned_in.astype(BF)
    first_half[...] = (turned_in.T * 0.5).astype(BF)
    second_t[...] = turned_out.astype(BF)
    second_half[...] = (turned_out.T * 0.5).astype(BF)
    bias1[...] = jnp.broadcast_to(gate_in_bias[...].astype(F32) * 0.5, bias1.shape).T
    bias2[...] = lax.dot_general(
        order,
        jnp.broadcast_to(gate_out_bias[...], (BLK, PAIRS)),
        across,
        preferred_element_type=F32,
    )
    for copy in copies[: len(moved)]:
        copy.wait()
    copies[-1].start()

    def form(i, carry):
        start = pl.multiple_of((STAY + i * MOVE) * BLK, MOVE * BLK)
        project(features[pl.ds(start, MOVE * BLK), :], weight[...], vt, STAY + i * MOVE)
        return carry

    lax.fori_loop(0, (OWN - STAY) // MOVE, form, 0)
    for copy in copies[len(moved) : -1]:
        copy.wait()

    def users_of(shard):
        packed = arrived[jnp.minimum(shard, owners - 1), 0 : ROWS // 2, :]
        return jnp.concatenate([packed[:, :H], packed[:, H:]], axis=0)

    def items_of(slot):
        return vt[jnp.minimum(slot, OWN - 1)]

    def logits_of(ref, k):
        return jnp.concatenate(
            [
                jnp.concatenate(
                    [ref[u * K : (u + 1) * K, b * BLK : (b + 1) * BLK] for b in range(K)],
                    axis=0,
                )
                for u in range(TILE_USERS * k, TILE_USERS * (k + 1))
            ],
            axis=1,
        )

    def stages(n, even):
        odd = 1 - even
        start_slot, start_shard = entry_slot[n + 2], entry_shard[n + 2]
        middle_shard, middle_start = entry_shard[n + 1], entry_start[n + 1]
        end_slot, end_shard = entry_slot[n], entry_shard[n]
        meta = arrived[jnp.minimum(middle_shard, owners - 1), ROWS // 2 : ROWS // 2 + 16, :]
        meta = meta.astype(F32)
        offset = meta[:, 0:16] * BLK + meta[:, 16:32] - middle_start.astype(F32)

        def scores():
            logits[even][...] = jnp.dot(
                users_of(start_shard), items_of(start_slot), preferred_element_type=F32
            )

        def forward(k):
            columns = slice(k * tile, (k + 1) * tile)
            h = jnp.dot(
                first_half[...],
                logits_of(logits[even], k).astype(BF),
                preferred_element_type=F32,
            ) + jnp.concatenate([bias1[...]] * TILE_USERS, axis=1)
            t = jnp.tanh(h)
            q = 1.0 + t
            silu = h * q
            hidden[even][:, columns] = silu.astype(BF)
            slope[even][:, columns] = q + silu * (1.0 - t)

        def mix(k):
            columns = slice(k * tile, (k + 1) * tile)
            users = range(TILE_USERS * k, TILE_USERS * (k + 1))
            y = jnp.concatenate(
                [
                    jnp.max(
                        jnp.where(offset[:, u : u + 1] == lane, 1.0, 0.0), axis=0, keepdims=True
                    )
                    for u in users
                ],
                axis=1,
            )
            gate = jnp.dot(
                second_t[...], hidden[odd][:, columns], preferred_element_type=F32
            ) + jnp.concatenate([bias2[...]] * TILE_USERS, axis=1)
            e = jnp.exp(gate)
            lk = logits_of(logits[odd], k)
            inverse = 1.0 / jnp.sum(e, axis=0, keepdims=True)
            score = jnp.sum(e * lk, axis=0, keepdims=True) * inverse
            score_grad = 0.5 + 0.5 * jnp.tanh(0.5 * score) - y
            weighted = e * (score_grad * inverse)
            weights[odd][:, columns] = weighted
            return (weighted * (lk - score)).astype(BF)

        def gate_back(k, logit_grad):
            columns = slice(k * tile, (k + 1) * tile)
            hidden_grad = jnp.dot(second_half[...], logit_grad, preferred_element_type=F32)
            back[odd][:, columns] = (hidden_grad * slope[odd][:, columns]).astype(BF)

        def pair_back(k):
            columns = slice(k * tile, (k + 1) * tile)
            pg = jnp.dot(first[...], back[even][:, columns], preferred_element_type=F32)
            pg = pg + weights[even][:, columns]
            rows = slice(K * TILE_USERS * k, K * TILE_USERS * (k + 1))
            for b in range(K):
                pair_grad[even][rows, b * BLK : (b + 1) * BLK] = jnp.concatenate(
                    [
                        pg[b * K : (b + 1) * K, w * BLK : (w + 1) * BLK]
                        for w in range(TILE_USERS)
                    ],
                    axis=0,
                ).astype(BF)

        for k in range(tiles):
            pair_back(k)
        scores()
        logit_grads = [mix(k) for k in range(tiles)]
        pgv = pair_grad[even][...]
        deltas[end_shard] += lax.dot_general(
            pgv, items_of(end_slot), (((1,), (1,)), ((), ())), preferred_element_type=F32
        )
        grads[end_slot] += jnp.dot(users_of(end_shard).T, pgv, preferred_element_type=F32)
        for k in range(tiles):
            forward(k)
            gate_back(k, logit_grads[k])

    def step(i, carry):
        stages(2 * i, 0)
        stages(2 * i + 1, 1)
        return carry

    lax.fori_loop(0, (count + 3) // 2, step, 0)

    rows = keep.shape[1] - K
    scaling = 1.0 / math.sqrt(H)
    piece = USERS * K
    for c in range(2 * USERS):
        columns = slice(c * H, (c + 1) * H)
        first_row = 2 * piece * (c // USERS) + K * (c % USERS)
        keep[:, rows:, columns] = (
            deltas[0:owners, first_row : first_row + K, :] * scaling
        ).astype(BF)
        first_row = first_row + piece
        send[:, rows:, columns] = (
            deltas[0:owners, first_row : first_row + K, :] * scaling
        ).astype(BF)
    copies[-1].wait()
    blocks = 8

    def add(i, carry):
        left = jnp.concatenate(
            [
                jnp.concatenate(
                    [
                        grads[i * blocks + c, :, b * BLK : (b + 1) * BLK].astype(BF)
                        for b in range(K)
                    ],
                    axis=0,
                )
                for c in range(blocks)
            ],
            axis=1,
        )
        start = pl.multiple_of(i * blocks * BLK, blocks * BLK)
        product = jnp.dot(
            left, features[pl.ds(start, blocks * BLK), :], preferred_element_type=F32
        )

        @pl.when(i == 0)
        def _():
            total[...] = product

        @pl.when(i > 0)
        def _():
            total[...] += product

        return carry

    lax.fori_loop(0, OWN // blocks, add, 0)
    parity = group[0] & 1
    for part in range(total.shape[1] // BLK):
        turned = total[:, part * BLK : (part + 1) * BLK].T
        for c in range(BLK // (2 * rows)):
            lower = turned[2 * rows * c : 2 * rows * c + rows, :]
            upper = turned[2 * rows * c + rows : 2 * rows * (c + 1), :]
            owner = part * (BLK // (2 * rows)) + c
            keep[owner, 0:rows, :] = jnp.where(parity == 0, lower, upper).astype(BF)
            send[owner, 0:rows, :] = jnp.where(parity == 0, upper, lower).astype(BF)


def pair_terms(codes, group, arrived, vectors, features, gates):
    owners = codes.shape[0]
    width = features[0].shape[1]
    any_spec = pl.BlockSpec(memory_space=pl.ANY)
    columns = CIRCLE_USERS * BLK
    hidden = gates[0].shape[1]
    shape = (owners, width // (2 * owners) + K, E)
    smem = pl.BlockSpec(memory_space=pltpu.SMEM)

    def twice(shape, dtype):
        return [pltpu.VMEM(shape, dtype)] * 2

    return pl.pallas_call(
        pair_kernel,
        out_shape=(jax.ShapeDtypeStruct(shape, BF),) * 2,
        in_specs=[smem] * 2 + [any_spec] * 2 + [VMEM_SPEC] + [any_spec] * 9 + [VMEM_SPEC] * 4,
        out_specs=(VMEM_SPEC, VMEM_SPEC),
        scratch_shapes=[
            pltpu.VMEM((hidden, PAIRS), BF),
            pltpu.VMEM((PAIRS, hidden), BF),
            pltpu.VMEM((PAIRS, hidden), BF),
            pltpu.VMEM((hidden, PAIRS), BF),
            pltpu.VMEM((hidden, BLK), F32),
            pltpu.VMEM((PAIRS, BLK), F32),
            pltpu.VMEM(arrived.shape, BF),
            pltpu.VMEM((OWN, H, K * BLK), BF),
            pltpu.VMEM((OWN * BLK, width), BF),
            pltpu.VMEM((OWN + 1, H, K * BLK), F32),
            pltpu.VMEM((owners + 1, ROWS, H), F32),
            pltpu.VMEM((E, width), F32),
            pltpu.SMEM((owners * MOST + 8,), jnp.int32),
            pltpu.SMEM((owners * MOST + 8,), jnp.int32),
            pltpu.SMEM((owners * MOST + 8,), jnp.int32),
            pltpu.SemaphoreType.DMA((11,)),
        ]
        + twice((ROWS, K * BLK), F32)
        + twice((hidden, columns), BF)
        + twice((hidden, columns), F32)
        + twice((PAIRS, columns), F32)
        + twice((hidden, columns), BF)
        + twice((ROWS, K * BLK), BF),
        compiler_params=pltpu.CompilerParams(vmem_limit_bytes=58 << 20),
        cost_estimate=pl.CostEstimate(
            flops=40 << 30, bytes_accessed=16 << 20, transcendentals=1 << 24
        ),
        name="pairs",
    )(codes, group, arrived, *vectors, *features, *gates)


def split_product(left_bf16, right_f32):
    upper = right_f32.astype(BF)
    lower = (right_f32 - upper.astype(F32)).astype(BF)
    dims = (((0,), (0,)), ((), ()))
    first = lax.dot_general(left_bf16, upper, dims, preferred_element_type=F32)
    second = lax.dot_general(left_bf16, lower, dims, preferred_element_type=F32)
    return first + second


def shards(
    item_features,
    tower_weight,
    gate_in,
    gate_in_bias,
    gate_out,
    gate_out_bias,
    user_table,
    user_ids,
    positive_item,
    listed_owner,
    listed_slot,
):
    owner_count = lax.axis_size("shard")
    group = lax.axis_index("blk")
    halves = []
    for i, (stride, by) in enumerate(NEIGHBOURS):
        first = (STAY + i * MOVE + group % 2 * HALF) * BLK
        half = lax.dynamic_slice_in_dim(item_features, first, HALF * BLK, axis=0)
        halves.append(along(half, owner_count, stride, by))
    halves, tower_weight = lax.optimization_barrier((halves, tower_weight))
    moved = []
    for half in halves:
        moved += [half, swapped(half, 1)]
    listings = listed_slot.shape[0]
    owner_ids = listed_owner[:, 0]
    served_by = serving_device(owner_ids, listed_slot)
    order = jnp.arange(listings, dtype=jnp.int32)
    same_device = served_by[:, None] == served_by[None, :]
    earlier = order[None, :] < order[:, None]
    rank_within = jnp.sum(jnp.logical_and(same_device, earlier), axis=1)
    device_match = served_by[:, None] == jnp.arange(owner_count, dtype=jnp.int32)[None, :]
    place = group * listings + order
    column = jnp.arange(1 + 2 * MOST, dtype=jnp.int32)[None, :]
    value = jnp.where(
        column == 0,
        1,
        jnp.where(column == 1 + rank_within[:, None], listed_slot[:, None], 0)
        + jnp.where(column == 1 + MOST + rank_within[:, None], place[:, None], 0),
    )
    codes = jnp.sum(
        jnp.where(device_match[:, :, None], value[:, None, :], 0), axis=0
    ).astype(BF)

    row_match = user_ids[:, None] == jnp.arange(UTAB, dtype=jnp.int32)[None, :]
    user_rows = jnp.dot(row_match.astype(BF), user_table, preferred_element_type=F32)
    user_rows = (user_rows * (1.0 / math.sqrt(H))).astype(BF).reshape(USERS * K, H)
    positives = positive_item.T
    marks = jnp.concatenate([positives // BLK, positives % BLK], axis=1).astype(BF)
    own = jnp.concatenate([user_rows, jnp.pad(marks, ((0, 0), (0, H - 2 * USERS)))], axis=0)
    pieces = [own] + [swapped(own, by) for by in range(1, GROUPS)]
    rows = [piece[: USERS * K] for piece in pieces]
    marks = [piece[USERS * K :] for piece in pieces]
    packed = jnp.concatenate(
        [jnp.concatenate(rows[0:2], axis=0), jnp.concatenate(rows[2:4], axis=0)], axis=1
    )
    meta = jnp.concatenate(
        [m[:, :USERS] for m in marks] + [m[:, USERS : 2 * USERS] for m in marks], axis=1
    )
    meta = jnp.pad(meta, ((0, 0), (0, 2 * H - 2 * CIRCLE_USERS)))
    common = jnp.concatenate([packed, meta], axis=0)
    sent = jnp.broadcast_to(common[None], (owner_count,) + common.shape)
    codes = jnp.pad(
        codes[:, None, :],
        ((0, 0), (ROWS // 2, 15), (2 * CIRCLE_USERS, 2 * H - 2 * CIRCLE_USERS - 1 - 2 * MOST)),
    )
    arrived = lax.all_to_all(sent + codes, "shard", split_axis=0, concat_axis=0, tiled=True)
    asked = arrived[:, ROWS // 2, 2 * CIRCLE_USERS : 2 * CIRCLE_USERS + 1 + 2 * MOST].astype(jnp.int32)

    vectors = (tower_vectors(tower_weight, item_features), tower_weight)
    gates = (gate_in, gate_in_bias[None, :], gate_out.T, gate_out_bias[None, :])
    keep, send = pair_terms(
        asked, group[None], arrived, vectors, (item_features, *moved), gates
    )
    terms = (keep.astype(F32) + swapped(send, 1).astype(F32)).astype(BF)
    terms = lax.all_to_all(terms, "shard", split_axis=0, concat_axis=0, tiled=True)
    sums = jnp.sum(terms.astype(F32), axis=0)
    rows = sums.shape[0] - K
    half = sums[:rows]
    from_1, from_2, from_3 = swapped(half, 1), swapped(sums, 2), swapped(half, 3)
    mine = half + from_2[:rows]
    other = from_1 + from_3
    even = group % 2 == 0
    tower_gradient = jnp.concatenate(
        [jnp.where(even, mine, other), jnp.where(even, other, mine)], axis=0
    )
    user_delta = sums[rows:, : USERS * H] + from_2[rows:, USERS * H :]
    user_delta = user_delta.reshape(K, USERS, H).transpose(1, 0, 2).reshape(USERS, E)
    user_gradient = split_product(row_match.astype(BF), user_delta)
    return (tower_gradient, user_gradient)


def solution(mesh):
    return jax.shard_map(
        shards,
        mesh=mesh,
        in_specs=(
            P("shard", None),
            P(),
            P(),
            P(),
            P(),
            P(),
            P(("blk", "shard"), None),
            P(("blk", "shard")),
            P(("blk", "shard"), None),
            P(("blk", "shard"), None),
            P(("blk", "shard")),
        ),
        out_specs=(P("shard", None), P(("blk", "shard"), None)),
        check_vma=False,
    )
```
